256 devices in a mesh: tm: 32 (over y, x, core), freq: 8 (over z).
Axes of the slice: x: 4, y: 4, z: 8, core: 2. Of those that a mesh axis runs over, the one named last changes fastest.
Arguments:
- increments: float32 [4096, 4, 128], P('tm'), may hold values from -6 to 6
- projections: float32 [128, 3, 4096], P(None, None, 'freq'), may hold values from -0.5 to 0.5
- phases: float32 [3, 4096], P(None, 'freq'), may hold values from -3.140625 to 3.140625
- groups: int32 [4], replicated, may hold values from 0 to 1, as said below
Outputs:
- grad_increments: float32 [4096, 4, 128], P(('tm', 'freq'))
- grad_projections: float32 [128, 3, 4096], P('tm', None, 'freq')
The draws below stay inside these ranges and needn't reach their ends.
Inputs may be any that keep to these rules, and one draw needn't show every extreme that they name: `groups`: exactly 2 sequences have 1.
All inputs are finite; a program needn't handle non-finite values.
Results may differ from the reference program's by a relative error of at most 0.0003.
Values sent between devices are 32-bit elements; how exact they have to be, the bound alone decides.
A program may use at most 64 MiB of HBM per device.

```python
import math
import jax
import jax.numpy as jnp
from jax import lax

CH = 128
FREQS = 4096
LEVELS = 3
BATCH = 4
LENGTH = 4096
N_FREQ = 8


def draw_groups(key, part):
    order = jax.random.permutation(key, BATCH)
    return (order < BATCH // 2).astype(jnp.int32)


def levels(rng, extent, cuts, least, largest):
    def one(position, parts):
        heights = jax.random.uniform(jax.random.fold_in(jax.random.fold_in(rng, 6), position), (parts,), jnp.float32, least / len(cuts), largest / len(cuts))
        return jnp.repeat(jnp.exp(heights), extent[position] // parts).reshape((-1,) + (1,) * (len(extent) - position - 1))

    level = one(*cuts[0])
    for cut in cuts[1:]:
        level = level * one(*cut)
    return level


def centred(own_key, shape, scale, reach, pieces=(), held_as=jnp.bfloat16):
    entries = scale * jax.random.normal(own_key, shape, jnp.float32)
    if pieces:
        entries = entries * levels(own_key, shape, pieces, -0.22, 0.18)
    return jnp.clip(entries, -reach, reach).astype(held_as)


def setup_inputs(seed: int = 0) -> dict:
    key_of = jax.random.split(jax.random.key(seed), 5)
    return {
        "increments": centred(key_of[0], (LENGTH, BATCH, CH), 1.0, 6.0, ((0, 32),), jnp.float32),
        "projections": centred(key_of[1], (CH, LEVELS, FREQS), CH ** -0.5, 0.5, ((2, 8),), jnp.float32),
        "phases": jnp.clip(jax.random.uniform(key_of[2], (LEVELS, FREQS), jnp.float32, -3.140625, 3.140625), -3.140625, 3.140625),
        "groups": draw_groups(jax.random.fold_in(key_of[4], 71), 0),
    }


highest = lax.Precision.HIGHEST

def before_sum(values):
    return jnp.cumsum(values, axis=0) - values

def after_sum(values):
    return lax.optimization_barrier(jnp.sum(values, axis=0, keepdims=True)) - jnp.cumsum(values, axis=0)

def reference(increments, projections, phases, groups):
    length, batch, chans = increments.shape
    amplitude = math.sqrt(2.0 / length)
    set_weight = jnp.where(groups == 1, 2.0 / batch, -2.0 / batch).astype(jnp.float32)[:, None]
    width = FREQS // N_FREQ
    block_proj = projections.reshape(chans, LEVELS, N_FREQ, width).transpose(2, 0, 1, 3)
    block_phase = phases.reshape(LEVELS, N_FREQ, width).transpose(1, 0, 2)

    def one_block(running, operands):
        proj_block, phase_block = operands
        angles = [jnp.einsum('tbc,cf->tbf', increments, proj_block[:, degree, :], precision=highest) + phase_block[degree][None, None, :] for degree in range(3)]
        waves = [amplitude * jnp.cos(angle) for angle in angles]
        front1 = before_sum(waves[0])
        term2 = front1 * waves[1]
        front2 = before_sum(term2)
        term3 = front2 * waves[2]
        totals = [lax.optimization_barrier(jnp.sum(waves[0], axis=0)), lax.optimization_barrier(jnp.sum(term2, axis=0)), lax.optimization_barrier(jnp.sum(term3, axis=0))]
        seeds = [2.0 * set_weight * lax.optimization_barrier(jnp.sum(set_weight * total, axis=0))[None, :] for total in totals]
        adjoint1 = seeds[1][None] + seeds[2][None] * after_sum(waves[2])
        adjoint0 = seeds[0][None] + after_sum(adjoint1 * waves[1])
        dirs = [adjoint0, adjoint1 * front1, seeds[2][None] * front2]
        slopes = [-amplitude * jnp.sin(angles[degree]) * dirs[degree] for degree in range(3)]
        grads = jnp.stack([jnp.einsum('tbc,tbf->cf', increments, slope, precision=highest) for slope in slopes], axis=1)
        update = running
        for degree in range(3):
            update = update + jnp.einsum('tbf,cf->tbc', slopes[degree], proj_block[:, degree, :], precision=highest)
        return (update, grads)
    start = jnp.zeros(increments.shape, jnp.float32)
    grad_increments, grads = lax.scan(one_block, start, (block_proj, block_phase))
    grad_projections = grads.transpose(1, 2, 0, 3).reshape(chans, LEVELS, FREQS)
    return (grad_increments, grad_projections)
```

```python
import functools
import math

import jax
import jax.numpy as jnp
from jax import lax
from jax.experimental import pallas as pl
from jax.experimental.pallas import tpu as pltpu
from jax.sharding import PartitionSpec as P

MESH = pl.DeviceIdType.MESH
F32 = jnp.float32
BF16 = jnp.bfloat16
TURN = 1.0 / (2.0 * math.pi)

SIN_POLY = (3.14159264, -5.16771008, 2.55007752, -0.59829129, 0.07765766)
COS_POLY = (1.0, -4.93480214, 4.05870916, -1.335212, 0.23493731, -0.02439632)

GRIDS = {32: (4, 4), 8: (2, 2)}

W0, W1, W2, A01, A12, A012 = range(6)


def halves(value):
    high = value.astype(BF16)
    return high, (value - high.astype(F32)).astype(BF16)


def dot(left, right):
    return jnp.dot(left, right, preferred_element_type=F32)


def dot_nt(left, right):
    return lax.dot_general(left, right, (((1,), (1,)), ((), ())), preferred_element_type=F32)


def poly(coefs, z):
    value = coefs[-1] * z + coefs[-2]
    for coef in coefs[-3::-1]:
        value = value * z + coef
    return value


def join(early, late):
    return [
        early[W0] + late[W0],
        early[W1] + late[W1],
        early[W2] + late[W2],
        early[A01] + late[A01] + early[W0] * late[W1],
        early[A12] + late[A12] + early[W1] * late[W2],
        early[A012] + late[A012] + early[A01] * late[W2] + early[W0] * late[A12],
    ]


def masked(tiles, keep):
    return [tile * keep for tile in tiles]


def around(buffer, count, place):
    members = [[buffer[k, q] for q in range(6)] for k in range(count)]
    total = members[0]
    for k in range(1, count):
        total = join(total, members[k])
    before = masked(members[0], jnp.where(place > 0, 1.0, 0.0).astype(F32))
    for k in range(1, count - 1):
        before = join(before, masked(members[k], jnp.where(place > k, 1.0, 0.0).astype(F32)))
    after = masked(members[1], jnp.where(place < 1, 1.0, 0.0).astype(F32))
    for k in range(2, count):
        after = join(after, masked(members[k], jnp.where(place < k, 1.0, 0.0).astype(F32)))
    return before, after, total


def kernel(
    sizes, inc_ref, proj_ref, phase_ref, group_ref, gi_out, gp_out,
    xl, xt, pr, pn, yb, wb, whl, fb, sh, sl, tri,
    summ, summ_in, xbuf, ybuf, coef, coef_send,
    gp, gp_in, gs, r1, t1, r2, fin, fin_in, gi, gi_in,
    pair_send, pair_recv, x_send, x_recv, y_send, y_recv, u_send, u_recv, v_send, v_recv, z_send, z_recv,
):
    ny, nx, nz, length = sizes
    steps, batch, chans, width = 128, 4, 128, 512
    half = width // 2
    rows = steps * batch
    strip = chans // (nx * ny)
    part = steps // nz
    amplitude = math.sqrt(2.0 / length)
    root = math.sqrt(2.0 * amplitude)
    sin_poly = [root * a for a in SIN_POLY]
    cos_poly = [-root * a for a in COS_POLY]

    tm, z = lax.axis_index("tm"), lax.axis_index("freq")
    core = lax.rem(tm, 2)
    x = lax.rem(tm // 2, nx)
    y = tm // (2 * nx)
    other = 1 - core
    pair = (tm + 1 - 2 * core, z)

    def along_x(k):
        return (y * (2 * nx) + k * 2 + core, z)

    def along_y(k):
        return (k * (2 * nx) + x * 2 + core, z)

    u, v = other * x + core * y, other * y + core * x

    def along_u(k):
        return (other * (y * (2 * nx) + k * 2) + core * (k * (2 * nx) + x * 2) + core, z)

    def along_v(k):
        return (other * (k * (2 * nx) + x * 2) + core * (y * (2 * nx) + k * 2) + core, z)

    def next_of(place, d, count):
        return lax.rem(place + d, count)

    barrier = pltpu.get_barrier_semaphore()
    peers = [pair]
    peers += [along_x(next_of(x, d, nx)) for d in range(1, nx)]
    peers += [along_y(next_of(y, d, ny)) for d in range(1, ny)]
    peers += [(tm, next_of(z, d, nz)) for d in range(1, nz)]
    for peer in peers:
        pl.semaphore_signal(barrier, inc=1, device_id=peer, device_id_type=MESH)

    def remote(src, dst, send, recv, peer):
        copy = pltpu.make_async_remote_copy(
            src_ref=src, dst_ref=dst, send_sem=send, recv_sem=recv, device_id=peer, device_id_type=MESH
        )
        copy.start()
        return copy

    for b in range(batch):
        block = inc_ref[pl.ds(b, steps, stride=batch), :]
        x1 = block.astype(BF16)
        left = block - x1.astype(F32)
        x2 = left.astype(BF16)
        x3 = (left - x2.astype(F32)).astype(BF16)
        at = slice(b * steps, (b + 1) * steps)
        for k, piece in enumerate((x1, x2, x1, x2, x3, x1)):
            xl[at, k * chans : (k + 1) * chans] = piece
        flip = block.T
        high, low = halves(flip)
        xt[0:chans, at] = high
        xt[chans : 2 * chans, at] = low

    row = lax.broadcasted_iota(jnp.int32, (steps, steps), 0)
    col = lax.broadcasted_iota(jnp.int32, (steps, steps), 1)
    lower = jnp.where(col < row, 1.0, 0.0).astype(BF16)
    upper = jnp.where(col > row, 1.0, 0.0).astype(BF16)
    for k in range(2):
        tri[0:steps, k * steps : (k + 1) * steps] = lower
        tri[steps : 2 * steps, k * steps : (k + 1) * steps] = upper

    def split_projections(i, carry):
        m, h = i // 2, lax.rem(i, 2)
        at = pl.ds(pl.multiple_of(h * half, half), half)
        block = proj_ref[m, :, at]
        high, low = halves(block)
        pn[m, 0:chans, at] = high
        pn[m, chans : 2 * chans, at] = low
        block = block * TURN
        p1 = block.astype(BF16)
        left = block - p1.astype(F32)
        p2 = left.astype(BF16)
        p3 = (left - p2.astype(F32)).astype(BF16)
        for k, piece in enumerate((p1, p1, p2, p2, p1, p3)):
            pr[m, k * chans : (k + 1) * chans, at] = piece
        return carry

    lax.fori_loop(0, 6, split_projections, 0)

    for m in range(3):
        yb[m * rows : (m + 1) * rows, :] = dot(xl[...], pr[m])
        shift = phase_ref[m : m + 1, :] * TURN

        def waves(i, carry, m=m, shift=shift):
            at = pl.ds(pl.multiple_of(m * rows + i * 16, 16), 16)
            turns = yb[at, :] + shift
            f = turns - jnp.round(turns)
            f2 = f * f
            s = f * poly(sin_poly, f2)
            c = poly(cos_poly, f2)
            w = amplitude - s * s
            wb[at, :] = w
            yb[at, :] = s * c
            high, low = halves(w)
            b, t = i // 8, lax.rem(i, 8)
            start = pl.multiple_of(b * (2 * steps) + t * 16, 16)
            whl[m, pl.ds(start, 16), :] = high
            whl[m, pl.ds(start + steps, 16), :] = low
            return carry

        lax.fori_loop(0, rows // 16, waves, 0)

    def local_sums(h, carry):
        at = pl.ds(pl.multiple_of(h * half, half), half)

        def put(q, b, value):
            total = jnp.sum(value, axis=0, keepdims=True)
            for l in range(2):
                summ[h, q, l * batch + b : l * batch + b + 1, :] = total[:, l * 128 : (l + 1) * 128]

        for b in range(batch):
            here = slice(b * steps, (b + 1) * steps)
            pair_rows = slice(b * 2 * steps, (b + 1) * 2 * steps)
            w0 = wb[b * steps : (b + 1) * steps, at]
            w1 = wb[rows + b * steps : rows + (b + 1) * steps, at]
            w2 = wb[2 * rows + b * steps : 2 * rows + (b + 1) * steps, at]
            put(W0, b, w0)
            put(W1, b, w1)
            put(W2, b, w2)
            b0 = dot(tri[0:steps, :], whl[0, pair_rows, at])
            fb[0, here, at] = b0
            both = dot(tri[...], whl[1, pair_rows, at])
            fb[1, here, at] = both[0:steps]
            fb[2, here, at] = both[steps : 2 * steps]
            a2 = dot(tri[steps : 2 * steps, :], whl[2, pair_rows, at])
            fb[3, here, at] = a2
            p = b0 * w1
            put(A01, b, p)
            b01 = dot(tri[0:steps, :], jnp.concatenate(halves(p), axis=0))
            fb[4, here, at] = b01
            put(A012, b, b01 * w2)
            q = a2 * w1
            put(A12, b, q)
            fb[5, here, at] = dot(tri[steps : 2 * steps, :], jnp.concatenate(halves(q), axis=0))
        return carry

    lax.fori_loop(0, 2, local_sums, 0)

    pl.semaphore_wait(barrier, len(peers))
    copies = []
    copy = remote(summ.at[other], summ_in, pair_send.at[0], pair_recv.at[0], pair)
    copies.append(copy)
    copy.wait_recv()
    mine = [summ[core, q] for q in range(6)]
    theirs = [summ_in[q] for q in range(6)]
    first = jnp.where(core == 0, 1.0, 0.0).astype(F32)
    core0 = [a * first + b * (1.0 - first) for a, b in zip(mine, theirs)]
    core1 = [b * first + a * (1.0 - first) for a, b in zip(mine, theirs)]
    for q, tile in enumerate(join(core0, core1)):
        xbuf[x, q] = tile
    for d in range(1, nx):
        k = next_of(x, d, nx)
        copies.append(remote(xbuf.at[x], xbuf.at[x], x_send.at[k], x_recv.at[x], along_x(k)))
    for d in range(1, nx):
        k = next_of(x, d, nx)
        pltpu.make_async_copy(xbuf.at[k], xbuf.at[k], x_recv.at[k]).wait()
    before_x, after_x, total = around(xbuf, nx, x)
    for q, tile in enumerate(total):
        ybuf[y, q] = tile
    for d in range(1, ny):
        k = next_of(y, d, ny)
        copies.append(remote(ybuf.at[y], ybuf.at[y], y_send.at[k], y_recv.at[y], along_y(k)))
    for d in range(1, ny):
        k = next_of(y, d, ny)
        pltpu.make_async_copy(ybuf.at[k], ybuf.at[k], y_recv.at[k]).wait()
    before_y, after_y, total = around(ybuf, ny, y)
    before = join(before_y, before_x)
    after = join(after_x, after_y)
    middle = join(before, core0)
    tail = join(core1, after)

    sub = lax.broadcasted_iota(jnp.int32, (8, 128), 0)
    weight = jnp.zeros((8, 128), F32)
    for b in range(batch):
        sign = jnp.where(group_ref[b] == 1, 2.0 / batch, -2.0 / batch).astype(F32)
        weight = jnp.where(lax.rem(sub, batch) == b, sign, weight)
    seeds = []
    for q in (W0, A01, A012):
        product = weight * total[q]
        gaps = []
        for l in range(2):
            gap = product[l * batch : l * batch + 1]
            for b in range(1, batch):
                gap = gap + product[l * batch + b : l * batch + b + 1]
            gaps.append(jnp.broadcast_to(gap, (8, 128)))
        seeds.append(2.0 * weight * jnp.where(sub < batch, gaps[0], gaps[1]))

    def coefs(ahead, behind):
        tail2 = seeds[1] * behind[W1] + seeds[2] * behind[A12]
        return [seeds[0] + tail2, seeds[1] + seeds[2] * behind[W2], seeds[2], ahead[W0], ahead[A01]]

    of_core0, of_core1 = coefs(before, tail), coefs(middle, after)
    for k in range(5):
        coef_send[k] = of_core1[k] * first + of_core0[k] * (1.0 - first)
        coef[core, k] = of_core0[k] * first + of_core1[k] * (1.0 - first)
    copy = remote(coef_send, coef.at[core], pair_send.at[1], pair_recv.at[1], pair)
    copies.append(copy)
    copy.wait_recv()

    def slopes(h, carry):
        for l in range(2):
            at = pl.ds(pl.multiple_of(h * half + l * 128, 128), 128)
            for b in range(batch):
                line = slice(l * batch + b, l * batch + b + 1)
                c0, c1, s2, e1, e2 = [coef[h, k, line, :] for k in range(5)]
                for t in range(0, steps, 64):
                    r = b * steps + t
                    here = slice(r, r + 64)
                    b0, b1, a1, a2, b01, q = [fb[k, here, at] for k in range(6)]
                    values = (
                        yb[r : r + 64, at] * (c0 + c1 * a1 + s2 * q),
                        yb[rows + r : rows + r + 64, at] * ((c1 + s2 * a2) * (e1 + b0)),
                        yb[2 * rows + r : 2 * rows + r + 64, at] * (s2 * (e2 + e1 * b1 + b01)),
                    )
                    for m in range(3):
                        high, low = halves(values[m])
                        sh[m, here, at] = high
                        sl[m, here, at] = low
        return carry

    lax.fori_loop(0, 2, slopes, 0)

    for b in range(batch):
        here = slice(b * steps, (b + 1) * steps)
        total = jnp.zeros((steps, chans), F32)
        for m in range(3):
            wide = dot_nt(sh[m, here, :], pn[m])
            total = total + wide[:, 0:chans] + wide[:, chans : 2 * chans] + dot_nt(sl[m, here, :], pn[m, 0:chans, :])
        gi[b] = total
    gi_copies = []
    for d in range(nz - 1, 0, -1):
        k = next_of(z, d, nz)
        src = gi.at[:, pl.ds(pl.multiple_of(k * part, part), part), :]
        gi_copies.append(remote(src, gi_in.at[z], z_send.at[k], z_recv.at[z], (tm, k)))

    def frequency_gradient(h):
        at = pl.ds(pl.multiple_of(h * half, half), half)
        for m in range(3):
            wide = dot(xt[...], sh[m, :, at])
            low = dot(xt[0:chans, :], sl[m, :, at])
            gp[h, :, m * half : (m + 1) * half] = wide[0:chans] + wide[chans : 2 * chans] + low

    frequency_gradient(other)
    pair_copy = remote(gp.at[other], gp_in, pair_send.at[2], pair_recv.at[2], pair)
    copies.append(pair_copy)
    frequency_gradient(core)
    pair_copy.wait_recv()
    for iy in range(ny):
        for ix in range(nx):
            at = slice((iy * nx + ix) * strip, (iy * nx + ix + 1) * strip)
            tile = gp[core, at, :] + gp_in[at, :]
            gs[other * ix + core * iy, other * iy + core * ix] = tile
    for d in range(1, nx):
        k = next_of(u, d, nx)
        copies.append(remote(gs.at[k], r1.at[u], u_send.at[k], u_recv.at[u], along_u(k)))
    r1[u] = gs[u]
    for d in range(1, nx):
        k = next_of(u, d, nx)
        pltpu.make_async_copy(r1.at[k], r1.at[k], u_recv.at[k]).wait()
    for j in range(ny):
        tile = r1[0, j]
        for k in range(1, nx):
            tile = tile + r1[k, j]
        t1[j] = tile
    for d in range(1, ny):
        k = next_of(v, d, ny)
        copies.append(remote(t1.at[k], r2.at[v], v_send.at[k], v_recv.at[v], along_v(k)))
    r2[v] = t1[v]
    for d in range(1, ny):
        k = next_of(v, d, ny)
        pltpu.make_async_copy(r2.at[k], r2.at[k], v_recv.at[k]).wait()
    tile = r2[0]
    for k in range(1, ny):
        tile = tile + r2[k]
    keep = strip // 2
    fin[0] = tile
    fin[1] = jnp.concatenate([tile[keep:], tile[:keep]], axis=0)
    copy = remote(fin.at[other], fin_in, pair_send.at[3], pair_recv.at[3], pair)
    copies.append(copy)

    for d in range(1, nz):
        k = next_of(z, d, nz)
        pltpu.make_async_copy(gi_in.at[k], gi_in.at[k], z_recv.at[k]).wait()
    own = gi[:, pl.ds(pl.multiple_of(z * part, part), part), :]
    gi_in[z] = own
    total = gi_in[0]
    for k in range(1, nz):
        total = total + gi_in[k]
    for b in range(batch):
        gi_out[pl.ds(b, part, stride=batch), :] = total[b]

    copy.wait_recv()
    for m in range(3):
        lanes = slice(m * half, (m + 1) * half)
        gp_out[m, :, pl.ds(pl.multiple_of(core * half, half), half)] = fin[core, 0:keep, lanes]
        gp_out[m, :, pl.ds(pl.multiple_of(other * half, half), half)] = fin_in[0:keep, lanes]
    for copy in copies + gi_copies:
        copy.wait_send()


def on_device(sizes, increments, projections, phases, groups):
    ny, nx, nz, _ = sizes
    steps, batch, chans = increments.shape
    width = projections.shape[2]
    strip = chans // (nx * ny)
    part = steps // nz
    rows = steps * batch
    half = width // 2
    vmem = pl.BlockSpec(memory_space=pltpu.VMEM)
    dma = pltpu.SemaphoreType.DMA
    gi, gp = pl.pallas_call(
        functools.partial(kernel, sizes),
        out_shape=(
            jax.ShapeDtypeStruct((part * batch, chans), F32),
            jax.ShapeDtypeStruct((3, strip // 2, width), F32),
        ),
        in_specs=[vmem, vmem, vmem, pl.BlockSpec(memory_space=pltpu.SMEM)],
        out_specs=(vmem, vmem),
        scratch_shapes=[
            pltpu.VMEM((rows, 6 * chans), BF16),
            pltpu.VMEM((2 * chans, rows), BF16),
            pltpu.VMEM((3, 6 * chans, width), BF16),
            pltpu.VMEM((3, 2 * chans, width), BF16),
            pltpu.VMEM((3 * rows, width), F32),
            pltpu.VMEM((3 * rows, width), F32),
            pltpu.VMEM((3, 2 * rows, width), BF16),
            pltpu.VMEM((6, rows, width), F32),
            pltpu.VMEM((3, rows, width), BF16),
            pltpu.VMEM((3, rows, width), BF16),
            pltpu.VMEM((2 * steps, 2 * steps), BF16),
            pltpu.VMEM((2, 6, 8, 128), F32),
            pltpu.VMEM((6, 8, 128), F32),
            pltpu.VMEM((nx, 6, 8, 128), F32),
            pltpu.VMEM((ny, 6, 8, 128), F32),
            pltpu.VMEM((2, 5, 8, 128), F32),
            pltpu.VMEM((5, 8, 128), F32),
            pltpu.VMEM((2, chans, 3 * half), F32),
            pltpu.VMEM((chans, 3 * half), F32),
            pltpu.VMEM((nx, ny, strip, 3 * half), F32),
            pltpu.VMEM((nx, ny, strip, 3 * half), F32),
            pltpu.VMEM((ny, strip, 3 * half), F32),
            pltpu.VMEM((ny, strip, 3 * half), F32),
            pltpu.VMEM((2, strip, 3 * half), F32),
            pltpu.VMEM((strip, 3 * half), F32),
            pltpu.VMEM((batch, steps, chans), F32),
            pltpu.VMEM((nz, batch, part, chans), F32),
            dma((4,)), dma((4,)),
            dma((nx,)), dma((nx,)),
            dma((ny,)), dma((ny,)),
            dma((nx,)), dma((nx,)),
            dma((ny,)), dma((ny,)),
            dma((nz,)), dma((nz,)),
        ],
        compiler_params=pltpu.CompilerParams(
            collective_id=0, has_side_effects=True, vmem_limit_bytes=60 << 20
        ),
    )(
        increments.reshape(rows, chans),
        projections.transpose(1, 0, 2),
        phases,
        groups,
    )
    return gi.reshape(part, batch, chans), gp.transpose(1, 0, 2)


def solution(mesh):
    tm, nz = mesh.shape["tm"], mesh.shape["freq"]
    ny, nx = GRIDS[tm]
    placed = (P("tm", None, None), P(None, None, "freq"), P(None, "freq"), P())
    return jax.shard_map(
        functools.partial(on_device, (ny, nx, nz, 128 * tm)),
        mesh=mesh,
        in_specs=placed,
        out_specs=(P(("tm", "freq"), None, None), P("tm", None, "freq")),
        check_vma=False,
    )
```

```python
import functools
import math

import jax
import jax.numpy as jnp
from jax import lax
from jax.experimental import pallas as pl
from jax.experimental.pallas import tpu as pltpu
from jax.sharding import PartitionSpec as P

MESH = pl.DeviceIdType.MESH
F32 = jnp.float32
BF16 = jnp.bfloat16
TURN = 1.0 / (2.0 * math.pi)

SIN_POLY = (3.14159264, -5.16771008, 2.55007752, -0.59829129, 0.07765766)
COS_POLY = (1.0, -4.93480214, 4.05870916, -1.335212, 0.23493731, -0.02439632)

NY, NX, NZ = 4, 4, 8
CHIPS = NY * NX
STEPS, BATCH, CHANS, WIDTH = 128, 4, 128, 512
LENGTH = STEPS * CHIPS * 2
HALF = WIDTH // 2
ROWS = STEPS * BATCH
PART = STEPS // NZ
LEVELS = 3

W0, W1, W2, A01, A12, A012 = range(6)


def halves(value):
    high = value.astype(BF16)
    return high, (value - high.astype(F32)).astype(BF16)


def dot(left, right):
    return jnp.dot(left, right, preferred_element_type=F32)


def dot_nt(left, right):
    return lax.dot_general(left, right, (((1,), (1,)), ((), ())), preferred_element_type=F32)


def poly(coefs, z):
    value = coefs[-1] * z + coefs[-2]
    for coef in coefs[-3::-1]:
        value = value * z + coef
    return value


def join(early, late):
    return [
        early[W0] + late[W0],
        early[W1] + late[W1],
        early[W2] + late[W2],
        early[A01] + late[A01] + early[W0] * late[W1],
        early[A12] + late[A12] + early[W1] * late[W2],
        early[A012] + late[A012] + early[A01] * late[W2] + early[W0] * late[A12],
    ]


def join_front(early, late):
    return {W0: early[W0] + late[W0], A01: early[A01] + late[A01] + early[W0] * late[W1]}


def join_back(early, late):
    return {
        W1: early[W1] + late[W1],
        W2: early[W2] + late[W2],
        A12: early[A12] + late[A12] + early[W1] * late[W2],
    }


def flag(condition):
    return jnp.where(condition, 1.0, 0.0).astype(F32)


def kernel(
    inc_hbm, proj_hbm, phase_ref, group_ref, gi_out, gp_out,
    inc_ref, proj_ref, xl, xt, pr, pt, fz, wb, whl, fb, sh, sl, tri,
    summ, summ_in, chips, coef, coef_send, gp_pair, gp_own, gp_in, gp_recv, gi, gi_in,
    in_sem, pair_send, pair_recv, c_send, c_recv, u_send, u_recv, z_send, z_recv,
):
    amplitude = math.sqrt(2.0 / LENGTH)
    root = math.sqrt(2.0 * amplitude)
    sin_poly = [root * a for a in SIN_POLY]
    cos_poly = [-root * a for a in COS_POLY]

    loads = [pltpu.make_async_copy(inc_hbm, inc_ref, in_sem.at[0])]
    loads += [pltpu.make_async_copy(proj_hbm.at[m], proj_ref.at[m], in_sem.at[1 + m]) for m in range(LEVELS)]
    for load in loads:
        load.start()

    tm, z = lax.axis_index("tm"), lax.axis_index("freq")
    core, chip = lax.rem(tm, 2), tm // 2
    other = 1 - core
    pair = (tm + 1 - 2 * core, z)

    def chip_at(d):
        return lax.rem(chip + d, CHIPS)

    def z_at(d):
        return lax.rem(z + d, NZ)

    barrier = pltpu.get_barrier_semaphore()
    peers = [pair] + [(2 * chip_at(d) + core, z) for d in range(1, CHIPS)] + [(tm, z_at(d)) for d in range(1, NZ)]
    for peer in peers:
        pl.semaphore_signal(barrier, inc=1, device_id=peer, device_id_type=MESH)

    def remote(src, dst, send, recv, peer):
        return pltpu.make_async_remote_copy(
            src_ref=src, dst_ref=dst, send_sem=send, recv_sem=recv, device_id=peer, device_id_type=MESH
        )

    row = lax.broadcasted_iota(jnp.int32, (STEPS, STEPS), 0)
    col = lax.broadcasted_iota(jnp.int32, (STEPS, STEPS), 1)
    lower = jnp.where(col < row, 1.0, 0.0).astype(BF16)
    upper = jnp.where(col > row, 1.0, 0.0).astype(BF16)
    for k in range(2):
        tri[0:STEPS, k * STEPS : (k + 1) * STEPS] = lower
        tri[STEPS : 2 * STEPS, k * STEPS : (k + 1) * STEPS] = upper

    loads[0].wait()
    for b in range(BATCH):
        block = inc_ref[pl.ds(b, STEPS, stride=BATCH), :]
        x1 = block.astype(BF16)
        left = block - x1.astype(F32)
        x2 = left.astype(BF16)
        x3 = (left - x2.astype(F32)).astype(BF16)
        at = slice(b * STEPS, (b + 1) * STEPS)
        for k, piece in enumerate((x1, x2, x1, x2, x3, x1)):
            xl[at, k * CHANS : (k + 1) * CHANS] = piece

    for m in range(LEVELS):
        loads[1 + m].wait()

        def split_projection(i, carry, m=m):
            at = pl.ds(pl.multiple_of(i * HALF, HALF), HALF)
            block = proj_ref[m, :, at] * TURN
            p1 = block.astype(BF16)
            left = block - p1.astype(F32)
            p2 = left.astype(BF16)
            p3 = (left - p2.astype(F32)).astype(BF16)
            for k, piece in enumerate((p1, p1, p2, p2, p1, p3)):
                pr[m, k * CHANS : (k + 1) * CHANS, at] = piece
            return carry

        lax.fori_loop(0, 2, split_projection, 0)

    pair_summ = remote(summ.at[other], summ_in, pair_send.at[0], pair_recv.at[0], pair)

    def local_sums(i, carry):
        h = lax.rem(core + 1 + i, 2)
        at = pl.ds(pl.multiple_of(h * HALF, HALF), HALF)

        def put(q, b, total):
            for l in range(2):
                summ[h, q, l * BATCH + b : l * BATCH + b + 1, :] = total[:, l * 128 : (l + 1) * 128]

        for m in range(LEVELS):
            turns_all = dot(xl[...], pr[m, :, at])
            shift = phase_ref[m : m + 1, at] * TURN
            for b in range(BATCH):
                total = jnp.zeros((16, HALF), F32)
                for t in range(0, STEPS, 16):
                    r = b * STEPS + t
                    turns = turns_all[r : r + 16] + shift
                    f = turns - jnp.round(turns)
                    fz[m, r : r + 16, at] = f
                    s = f * poly(sin_poly, f * f)
                    w = amplitude - s * s
                    total = total + w
                    if m == 1:
                        wb[r : r + 16, at] = w
                    high, low = halves(w)
                    whl[m, 2 * b * STEPS + t : 2 * b * STEPS + t + 16, at] = high
                    whl[m, (2 * b + 1) * STEPS + t : (2 * b + 1) * STEPS + t + 16, at] = low
                put(m, b, jnp.sum(total, axis=0, keepdims=True))
        for b in range(BATCH):
            here = slice(b * STEPS, (b + 1) * STEPS)
            both = slice(2 * b * STEPS, 2 * (b + 1) * STEPS)
            b0 = dot(tri[0:STEPS, :], whl[0, both, at])
            a2 = dot(tri[STEPS : 2 * STEPS, :], whl[2, both, at])
            fb[0, here, at] = b0
            fb[3, here, at] = a2
            sums = [jnp.zeros((16, HALF), F32)] * 3
            for t in range(0, STEPS, 16):
                w1 = wb[b * STEPS + t : b * STEPS + t + 16, at]
                p, a = b0[t : t + 16] * w1, a2[t : t + 16]
                sums = [sums[0] + p, sums[1] + a * w1, sums[2] + a * p]
            for q, total in zip((A01, A12, A012), sums):
                put(q, b, jnp.sum(total, axis=0, keepdims=True))

        @pl.when(i == 0)
        def _():
            pl.semaphore_wait(barrier, len(peers))
            pair_summ.start()

        return carry

    lax.fori_loop(0, 2, local_sums, 0)

    pair_summ.wait_recv()
    mine = [summ[core, q] for q in range(6)]
    theirs = [summ_in[q] for q in range(6)]
    first = flag(core == 0)
    core0 = [a * first + b * (1.0 - first) for a, b in zip(mine, theirs)]
    core1 = [b * first + a * (1.0 - first) for a, b in zip(mine, theirs)]
    for q, tile in enumerate(join(core0, core1)):
        chips[chip, q] = tile
    chip_copies = []
    for d in range(1, CHIPS):
        k = chip_at(d)
        copy = remote(chips.at[chip], chips.at[chip], c_send.at[k], c_recv.at[chip], (2 * k + core, z))
        copy.start()
        chip_copies.append(copy)

    def scans(i, carry):
        at = pl.ds(pl.multiple_of(i * HALF, HALF), HALF)
        for b in range(BATCH):
            here = slice(b * STEPS, (b + 1) * STEPS)
            both = dot(tri[...], whl[1, 2 * b * STEPS : 2 * (b + 1) * STEPS, at])
            fb[1, here, at] = both[0:STEPS]
            fb[2, here, at] = both[STEPS : 2 * STEPS]
            w1 = wb[here, at]
            fb[4, here, at] = dot(tri[0:STEPS, :], jnp.concatenate(halves(fb[0, here, at] * w1), axis=0))
            fb[5, here, at] = dot(tri[STEPS : 2 * STEPS, :], jnp.concatenate(halves(fb[3, here, at] * w1), axis=0))
        return carry

    lax.fori_loop(0, 2, scans, 0)

    def sines(i, carry):
        at = pl.ds(pl.multiple_of(i * 16, 16), 16)
        for m in range(LEVELS):
            for l in range(0, WIDTH, HALF):
                f = fz[m, at, l : l + HALF]
                f2 = f * f
                fz[m, at, l : l + HALF] = f * poly(sin_poly, f2) * poly(cos_poly, f2)
        return carry

    lax.fori_loop(0, ROWS // 16, sines, 0)

    for h in range(2):
        for m in range(LEVELS):
            for l in range(2):
                lanes = slice(h * HALF + l * 128, h * HALF + (l + 1) * 128)
                high, low = halves(proj_ref[m, :, lanes].T)
                down = slice(m * HALF + l * 128, m * HALF + (l + 1) * 128)
                pt[h, down, 0:CHANS] = high
                pt[h, down, CHANS : 2 * CHANS] = low

    for order in range(2):
        place = lax.rem(row, 64)
        k = place // 4
        k = k + order * (1 - 2 * lax.rem(k, 2))
        channel = 8 * k + 4 * (row // 64) + lax.rem(place, 4)
        pick = jnp.where(col == channel, 1.0, 0.0).astype(BF16)
        for b in range(BATCH):
            at = slice(b * STEPS, (b + 1) * STEPS)
            high = dot_nt(pick, xl[at, 0:CHANS]).astype(BF16)
            low = dot_nt(pick, xl[at, CHANS : 2 * CHANS]).astype(BF16)
            for c in range(2):
                xt[order, c, 0:64, at] = high[64 * c : 64 * (c + 1)]
                xt[order, c, 64:128, at] = low[64 * c : 64 * (c + 1)]

    sub = lax.broadcasted_iota(jnp.int32, (8, 128), 0)
    weight = jnp.zeros((8, 128), F32)
    for b in range(BATCH):
        sign = jnp.where(group_ref[b] == 1, 2.0 / BATCH, -2.0 / BATCH).astype(F32)
        weight = jnp.where(lax.rem(sub, BATCH) == b, sign, weight)

    for d in range(1, CHIPS):
        k = chip_at(d)
        remote(chips.at[k], chips.at[k], c_send.at[k], c_recv.at[k], (2 * k + core, z)).wait_recv()
    members = [[chips[k, q] for q in range(6)] for k in range(CHIPS)]
    total = members[0]
    for k in range(1, CHIPS):
        total = join(total, members[k])
    zero = jnp.zeros((8, 128), F32)
    before = [zero] * 6
    for k in range(CHIPS - 1):
        keep = flag(chip > k)
        before = join_front(before, [tile * keep for tile in members[k]])
    after = [zero] * 6
    for k in range(1, CHIPS):
        keep = flag(chip < k)
        after = join_back(after, [tile * keep for tile in members[k]])
    middle = join_front(before, core0)
    tail = join_back(core1, after)

    seeds = []
    for q in (W0, A01, A012):
        product = weight * total[q]
        gaps = []
        for l in range(2):
            gap = product[l * BATCH : l * BATCH + 1]
            for b in range(1, BATCH):
                gap = gap + product[l * BATCH + b : l * BATCH + b + 1]
            gaps.append(jnp.broadcast_to(gap, (8, 128)))
        seeds.append(2.0 * weight * jnp.where(sub < BATCH, gaps[0], gaps[1]))

    def coefs(ahead, behind):
        tail2 = seeds[1] * behind[W1] + seeds[2] * behind[A12]
        return [seeds[0] + tail2, seeds[1] + seeds[2] * behind[W2], seeds[2], ahead[W0], ahead[A01]]

    of_core0, of_core1 = coefs(before, tail), coefs(middle, after)
    for k in range(5):
        coef_send[k] = of_core1[k] * first + of_core0[k] * (1.0 - first)
        coef[core, k] = of_core0[k] * first + of_core1[k] * (1.0 - first)
    pair_coef = remote(coef_send, coef.at[core], pair_send.at[1], pair_recv.at[1], pair)
    pair_coef.start()

    def slopes(h):
        for l in range(2):
            at = pl.ds(pl.multiple_of(h * HALF + l * 128, 128), 128)
            for b in range(BATCH):
                line = slice(l * BATCH + b, l * BATCH + b + 1)
                c0, c1, s2, e1, e2 = [coef[h, k, line, :] for k in range(5)]
                for t in range(0, STEPS, 64):
                    r = b * STEPS + t
                    here = slice(r, r + 64)
                    b0, b1, a1, a2, b01, q = [fb[k, here, at] for k in range(6)]
                    values = (
                        fz[0, here, at] * (c0 + c1 * a1 + s2 * q),
                        fz[1, here, at] * ((c1 + s2 * a2) * (e1 + b0)),
                        fz[2, here, at] * (s2 * (e2 + e1 * b1 + b01)),
                    )
                    for m in range(LEVELS):
                        high, low = halves(values[m])
                        lanes = slice(m * HALF + l * 128, m * HALF + (l + 1) * 128)
                        sh[h, here, lanes] = high
                        sl[h, here, lanes] = low

    def increments_part(h):
        wide = dot(sh[h], pt[h])
        return wide[:, 0:CHANS] + wide[:, CHANS : 2 * CHANS] + dot(sl[h], pt[h, :, 0:CHANS])

    def frequencies(c, out):
        parts = []
        for h in range(2):
            wide = dot(xt[h, c], sh[h])
            parts.append(wide[0:64] + wide[64:128] + dot(xt[h, c, 0:64, :], sl[h]))
        top = lax.broadcasted_iota(jnp.int32, (8, LEVELS * HALF), 0) < 4
        for j in range(CHIPS // 2):
            left, right = [part[8 * j : 8 * (j + 1)] for part in parts]
            out[2 * j] = jnp.where(top, left, right)
            out[2 * j + 1] = jnp.where(top, right, left)

    slopes(core)
    gi_own = increments_part(core)
    for b in range(BATCH):
        gi[b] = gi_own[b * STEPS : (b + 1) * STEPS]
    pair_coef.wait_recv()
    slopes(other)

    frequencies(other, gp_pair)
    pair_gp = remote(gp_pair, gp_in, pair_send.at[2], pair_recv.at[2], pair)
    pair_gp.start()
    frequencies(core, gp_own)
    gi_other = increments_part(other)
    for b in range(BATCH):
        gi[b] = gi[b] + gi_other[b * STEPS : (b + 1) * STEPS]
    z_copies = []
    for d in range(NZ - 1, 0, -1):
        k = z_at(d)
        src = gi.at[:, pl.ds(pl.multiple_of(k * PART, PART), PART), :]
        copy = remote(src, gi_in.at[z], z_send.at[k], z_recv.at[z], (tm, k))
        copy.start()
        z_copies.append(copy)
    pair_gp.wait_recv()
    gp_copies = []
    for d in range(1, CHIPS):
        k = chip_at(d)
        gp_own[k] = gp_own[k] + gp_in[k]
        copy = remote(gp_own.at[k], gp_recv.at[chip], u_send.at[k], u_recv.at[chip], (2 * k + core, z))
        copy.start()
        gp_copies.append(copy)
    gp_recv[chip] = gp_own[chip] + gp_in[chip]
    gi_in[z] = gi[:, pl.ds(pl.multiple_of(z * PART, PART), PART), :]

    for d in range(1, NZ):
        k = z_at(d)
        remote(gi_in.at[k], gi_in.at[k], z_send.at[k], z_recv.at[k], (tm, k)).wait_recv()
    total = gi_in[0]
    for k in range(1, NZ):
        total = total + gi_in[k]
    for b in range(BATCH):
        gi_out[pl.ds(b, PART, stride=BATCH), :] = total[b]

    for d in range(1, CHIPS):
        k = chip_at(d)
        remote(gp_recv.at[k], gp_recv.at[k], u_send.at[k], u_recv.at[k], (2 * k + core, z)).wait_recv()
    total = gp_recv[0]
    for k in range(1, CHIPS):
        total = total + gp_recv[k]
    swap = lax.rem(chip, 2)
    for m in range(LEVELS):
        lanes = slice(m * HALF, (m + 1) * HALF)
        gp_out[m, :, pl.ds(pl.multiple_of(swap * HALF, HALF), HALF)] = total[0:4, lanes]
        gp_out[m, :, pl.ds(pl.multiple_of((1 - swap) * HALF, HALF), HALF)] = total[4:8, lanes]
    for copy in [pair_summ, pair_coef, pair_gp] + chip_copies + z_copies + gp_copies:
        copy.wait_send()


def on_device(increments, projections, phases, groups):
    vmem = pl.BlockSpec(memory_space=pltpu.VMEM)
    hbm = pl.BlockSpec(memory_space=pl.ANY)
    dma = pltpu.SemaphoreType.DMA
    tile = (6, 8, 128)
    wide = LEVELS * HALF
    gi, gp = pl.pallas_call(
        kernel,
        out_shape=(
            jax.ShapeDtypeStruct((PART * BATCH, CHANS), F32),
            jax.ShapeDtypeStruct((LEVELS, CHANS // CHIPS // 2, WIDTH), F32),
        ),
        in_specs=[hbm, hbm, vmem, pl.BlockSpec(memory_space=pltpu.SMEM)],
        out_specs=(vmem, vmem),
        scratch_shapes=[
            pltpu.VMEM((ROWS, CHANS), F32),
            pltpu.VMEM((LEVELS, CHANS, WIDTH), F32),
            pltpu.VMEM((ROWS, 6 * CHANS), BF16),
            pltpu.VMEM((2, 2, CHANS, ROWS), BF16),
            pltpu.VMEM((LEVELS, 6 * CHANS, WIDTH), BF16),
            pltpu.VMEM((2, wide, 2 * CHANS), BF16),
            pltpu.VMEM((LEVELS, ROWS, WIDTH), F32),
            pltpu.VMEM((ROWS, WIDTH), F32),
            pltpu.VMEM((LEVELS, 2 * ROWS, WIDTH), BF16),
            pltpu.VMEM((6, ROWS, WIDTH), F32),
            pltpu.VMEM((2, ROWS, wide), BF16),
            pltpu.VMEM((2, ROWS, wide), BF16),
            pltpu.VMEM((2 * STEPS, 2 * STEPS), BF16),
            pltpu.VMEM((2, *tile), F32),
            pltpu.VMEM(tile, F32),
            pltpu.VMEM((CHIPS, *tile), F32),
            pltpu.VMEM((2, 5, 8, 128), F32),
            pltpu.VMEM((5, 8, 128), F32),
            pltpu.VMEM((CHIPS, 8, wide), F32),
            pltpu.VMEM((CHIPS, 8, wide), F32),
            pltpu.VMEM((CHIPS, 8, wide), F32),
            pltpu.VMEM((CHIPS, 8, wide), F32),
            pltpu.VMEM((BATCH, STEPS, CHANS), F32),
            pltpu.VMEM((NZ, BATCH, PART, CHANS), F32),
            dma((4,)),
            dma((3,)), dma((3,)),
            dma((CHIPS,)), dma((CHIPS,)),
            dma((CHIPS,)), dma((CHIPS,)),
            dma((NZ,)), dma((NZ,)),
        ],
        compiler_params=pltpu.CompilerParams(
            collective_id=0, has_side_effects=True, vmem_limit_bytes=60 << 20
        ),
    )(
        increments.reshape(ROWS, CHANS),
        projections.transpose(1, 0, 2),
        phases,
        groups,
    )
    return gi.reshape(PART, BATCH, CHANS), gp.transpose(1, 0, 2)


def solution(mesh):
    placed = (P("tm", None, None), P(None, None, "freq"), P(None, "freq"), P())
    return jax.shard_map(
        on_device,
        mesh=mesh,
        in_specs=placed,
        out_specs=(P(("tm", "freq"), None, None), P("tm", None, "freq")),
        check_vma=False,
    )
```

```python
import functools
import math

import jax
import jax.numpy as jnp
from jax import lax
from jax.experimental import pallas as pl
from jax.experimental.pallas import tpu as pltpu
from jax.sharding import PartitionSpec as P

MESH = pl.DeviceIdType.MESH
F32 = jnp.float32
BF16 = jnp.bfloat16
TURN = 1.0 / (2.0 * math.pi)

SIN_POLY = (3.14159264, -5.16771008, 2.55007752, -0.59829129, 0.07765766)
COS_POLY = (1.0, -4.93480214, 4.05870916, -1.335212, 0.23493731, -0.02439632)

NY, NX, NZ = 4, 4, 8
CHIPS = NY * NX
STEPS, BATCH, CHANS, WIDTH = 128, 4, 128, 512
LENGTH = STEPS * CHIPS * 2
HALF = WIDTH // 2
ROWS = STEPS * BATCH
PART = STEPS // NZ
LEVELS = 3


def ring(d, count):
    return min(d, count - d)


CHIP_ORDER = sorted(range(1, CHIPS), key=lambda d: -ring(d // NX, NY) - ring(d % NX, NX))
Z_ORDER = sorted(range(1, NZ), key=lambda d: -ring(d, NZ))

W0, W1, W2, A01, A12, A012 = range(6)


def halves(value):
    high = value.astype(BF16)
    return high, (value - high.astype(F32)).astype(BF16)


def dot(left, right):
    return jnp.dot(left, right, preferred_element_type=F32)


def dot_nt(left, right):
    return lax.dot_general(left, right, (((1,), (1,)), ((), ())), preferred_element_type=F32)


def poly(coefs, z):
    value = coefs[-1] * z + coefs[-2]
    for coef in coefs[-3::-1]:
        value = value * z + coef
    return value


def join(early, late):
    return [
        early[W0] + late[W0],
        early[W1] + late[W1],
        early[W2] + late[W2],
        early[A01] + late[A01] + early[W0] * late[W1],
        early[A12] + late[A12] + early[W1] * late[W2],
        early[A012] + late[A012] + early[A01] * late[W2] + early[W0] * late[A12],
    ]


def join_front(early, late):
    return {W0: early[W0] + late[W0], A01: early[A01] + late[A01] + early[W0] * late[W1]}


def join_back(early, late):
    return {
        W1: early[W1] + late[W1],
        W2: early[W2] + late[W2],
        A12: early[A12] + late[A12] + early[W1] * late[W2],
    }


def flag(condition):
    return jnp.where(condition, 1.0, 0.0).astype(F32)


def kernel(
    inc_hbm, proj_hbm, phase_hbm, group_hbm, gi_out, gp_out,
    inc_ref, proj_ref, phase_ref, group_ref, xl, xt, pr, pt, fz, wb, whl, fb, sh, sl, tri,
    summ, summ_in, chips, coef, coef_send, gp_half, gp_pair, gp_own, gp_in, gp_recv, gi, gi_in,
    in_sem, pair_send, pair_recv, g_send, g_recv, c_send, c_recv, u_send, u_recv, z_send, z_recv,
):
    amplitude = math.sqrt(2.0 / LENGTH)
    root = math.sqrt(2.0 * amplitude)
    sin_poly = [root * a for a in SIN_POLY]
    cos_poly = [-root * a for a in COS_POLY]

    loads = [pltpu.make_async_copy(inc_hbm, inc_ref, in_sem.at[0])]
    loads += [pltpu.make_async_copy(proj_hbm.at[m], proj_ref.at[m], in_sem.at[1 + m]) for m in range(LEVELS)]
    loads.append(pltpu.make_async_copy(phase_hbm, phase_ref, in_sem.at[4]))
    loads.append(pltpu.make_async_copy(group_hbm, group_ref, in_sem.at[5]))
    for load in loads:
        load.start()

    tm, z = lax.axis_index("tm"), lax.axis_index("freq")
    core, chip = lax.rem(tm, 2), tm // 2
    other = 1 - core
    pair = (tm + 1 - 2 * core, z)

    def chip_at(d):
        return lax.rem(chip // NX + d // NX, NY) * NX + lax.rem(lax.rem(chip, NX) + d % NX, NX)

    def z_at(d):
        return lax.rem(z + d, NZ)

    barrier = pltpu.get_barrier_semaphore()
    peers = [pair] + [(2 * chip_at(d) + core, z) for d in CHIP_ORDER] + [(tm, z_at(d)) for d in range(1, NZ)]
    for peer in peers:
        pl.semaphore_signal(barrier, inc=1, device_id=peer, device_id_type=MESH)

    def remote(src, dst, send, recv, peer):
        return pltpu.make_async_remote_copy(
            src_ref=src, dst_ref=dst, send_sem=send, recv_sem=recv, device_id=peer, device_id_type=MESH
        )

    row = lax.broadcasted_iota(jnp.int32, (STEPS, STEPS), 0)
    col = lax.broadcasted_iota(jnp.int32, (STEPS, STEPS), 1)
    lower = jnp.where(col < row, 1.0, 0.0).astype(BF16)
    upper = jnp.where(col > row, 1.0, 0.0).astype(BF16)
    for k in range(2):
        tri[0:STEPS, k * STEPS : (k + 1) * STEPS] = lower
        tri[STEPS : 2 * STEPS, k * STEPS : (k + 1) * STEPS] = upper

    loads[0].wait()
    for b in range(BATCH):
        block = inc_ref[pl.ds(b, STEPS, stride=BATCH), :]
        x1 = block.astype(BF16)
        left = block - x1.astype(F32)
        x2 = left.astype(BF16)
        x3 = (left - x2.astype(F32)).astype(BF16)
        at = slice(b * STEPS, (b + 1) * STEPS)
        for k, piece in enumerate((x1, x2, x1, x2, x3, x1)):
            xl[at, k * CHANS : (k + 1) * CHANS] = piece

    for m in range(LEVELS):
        loads[1 + m].wait()

        def split_projection(i, carry, m=m):
            at = pl.ds(pl.multiple_of(i * HALF, HALF), HALF)
            block = proj_ref[m, :, at] * TURN
            p1 = block.astype(BF16)
            left = block - p1.astype(F32)
            p2 = left.astype(BF16)
            p3 = (left - p2.astype(F32)).astype(BF16)
            for k, piece in enumerate((p1, p1, p2, p2, p1, p3)):
                pr[m, k * CHANS : (k + 1) * CHANS, at] = piece
            return carry

        lax.fori_loop(0, 2, split_projection, 0)

    loads[4].wait()
    loads[5].wait()

    pair_summ = remote(summ.at[other], summ_in, pair_send.at[0], pair_recv.at[0], pair)

    def local_sums(i, carry):
        h = lax.rem(core + 1 + i, 2)
        at = pl.ds(pl.multiple_of(h * HALF, HALF), HALF)

        def put(q, b, total):
            for l in range(2):
                summ[h, q, l * BATCH + b : l * BATCH + b + 1, :] = total[:, l * 128 : (l + 1) * 128]

        for m in range(LEVELS):
            turns_all = dot(xl[...], pr[m, :, at])
            shift = phase_ref[m : m + 1, at] * TURN
            for b in range(BATCH):
                total = jnp.zeros((16, HALF), F32)
                for t in range(0, STEPS, 16):
                    r = b * STEPS + t
                    turns = turns_all[r : r + 16] + shift
                    f = turns - jnp.round(turns)
                    fz[m, r : r + 16, at] = f
                    s = f * poly(sin_poly, f * f)
                    w = amplitude - s * s
                    total = total + w
                    if m == 1:
                        wb[r : r + 16, at] = w
                    high, low = halves(w)
                    whl[m, 2 * b * STEPS + t : 2 * b * STEPS + t + 16, at] = high
                    whl[m, (2 * b + 1) * STEPS + t : (2 * b + 1) * STEPS + t + 16, at] = low
                put(m, b, jnp.sum(total, axis=0, keepdims=True))
        for b in range(BATCH):
            here = slice(b * STEPS, (b + 1) * STEPS)
            both = slice(2 * b * STEPS, 2 * (b + 1) * STEPS)
            b0 = dot(tri[0:STEPS, :], whl[0, both, at])
            a2 = dot(tri[STEPS : 2 * STEPS, :], whl[2, both, at])
            fb[0, here, at] = b0
            fb[3, here, at] = a2
            sums = [jnp.zeros((16, HALF), F32)] * 3
            for t in range(0, STEPS, 16):
                w1 = wb[b * STEPS + t : b * STEPS + t + 16, at]
                p, a = b0[t : t + 16] * w1, a2[t : t + 16]
                sums = [sums[0] + p, sums[1] + a * w1, sums[2] + a * p]
            for q, total in zip((A01, A12, A012), sums):
                put(q, b, jnp.sum(total, axis=0, keepdims=True))

        @pl.when(i == 0)
        def _():
            pl.semaphore_wait(barrier, len(peers))
            pair_summ.start()

        return carry

    lax.fori_loop(0, 2, local_sums, 0)

    pair_summ.wait_recv()
    mine = [summ[core, q] for q in range(6)]
    theirs = [summ_in[q] for q in range(6)]
    first = flag(core == 0)
    core0 = [a * first + b * (1.0 - first) for a, b in zip(mine, theirs)]
    core1 = [b * first + a * (1.0 - first) for a, b in zip(mine, theirs)]
    for q, tile in enumerate(join(core0, core1)):
        chips[chip, q] = tile
    chip_copies = []
    for d in CHIP_ORDER:
        k = chip_at(d)
        copy = remote(chips.at[chip], chips.at[chip], c_send.at[k], c_recv.at[chip], (2 * k + core, z))
        copy.start()
        chip_copies.append(copy)

    def scans(i, carry):
        at = pl.ds(pl.multiple_of(i * HALF, HALF), HALF)
        for b in range(BATCH):
            here = slice(b * STEPS, (b + 1) * STEPS)
            both = dot(tri[...], whl[1, 2 * b * STEPS : 2 * (b + 1) * STEPS, at])
            fb[1, here, at] = both[0:STEPS]
            fb[2, here, at] = both[STEPS : 2 * STEPS]
            w1 = wb[here, at]
            fb[4, here, at] = dot(tri[0:STEPS, :], jnp.concatenate(halves(fb[0, here, at] * w1), axis=0))
            fb[5, here, at] = dot(tri[STEPS : 2 * STEPS, :], jnp.concatenate(halves(fb[3, here, at] * w1), axis=0))
        return carry

    lax.fori_loop(0, 2, scans, 0)

    def sines(i, carry):
        at = pl.ds(pl.multiple_of(i * 16, 16), 16)
        for m in range(LEVELS):
            for l in range(0, WIDTH, HALF):
                f = fz[m, at, l : l + HALF]
                f2 = f * f
                fz[m, at, l : l + HALF] = f * poly(sin_poly, f2) * poly(cos_poly, f2)
        return carry

    lax.fori_loop(0, ROWS // 16, sines, 0)

    for h in range(2):
        for m in range(LEVELS):
            for l in range(2):
                lanes = slice(h * HALF + l * 128, h * HALF + (l + 1) * 128)
                high, low = halves(proj_ref[m, :, lanes].T)
                down = slice(m * HALF + l * 128, m * HALF + (l + 1) * 128)
                pt[h, down, 0:CHANS] = high
                pt[h, down, CHANS : 2 * CHANS] = low

    for order in range(2):
        place = lax.rem(row, 64)
        k = place // 4
        k = k + order * (1 - 2 * lax.rem(k, 2))
        channel = 8 * k + 4 * (row // 64) + lax.rem(place, 4)
        pick = jnp.where(col == channel, 1.0, 0.0).astype(BF16)
        for b in range(BATCH):
            at = slice(b * STEPS, (b + 1) * STEPS)
            high = dot_nt(pick, xl[at, 0:CHANS]).astype(BF16)
            low = dot_nt(pick, xl[at, CHANS : 2 * CHANS]).astype(BF16)
            for c in range(2):
                xt[order, c, 0:64, at] = high[64 * c : 64 * (c + 1)]
                xt[order, c, 64:128, at] = low[64 * c : 64 * (c + 1)]

    sub = lax.broadcasted_iota(jnp.int32, (8, 128), 0)
    weight = jnp.zeros((8, 128), F32)
    for b in range(BATCH):
        sign = jnp.where(group_ref[b] == 1, 2.0 / BATCH, -2.0 / BATCH).astype(F32)
        weight = jnp.where(lax.rem(sub, BATCH) == b, sign, weight)

    for d in CHIP_ORDER:
        k = chip_at(d)
        remote(chips.at[k], chips.at[k], c_send.at[k], c_recv.at[k], (2 * k + core, z)).wait_recv()
    members = [[chips[k, q] for q in range(6)] for k in range(CHIPS)]
    total = members[0]
    for k in range(1, CHIPS):
        total = join(total, members[k])
    zero = jnp.zeros((8, 128), F32)
    before = [zero] * 6
    for k in range(CHIPS - 1):
        keep = flag(chip > k)
        before = join_front(before, [tile * keep for tile in members[k]])
    after = [zero] * 6
    for k in range(1, CHIPS):
        keep = flag(chip < k)
        after = join_back(after, [tile * keep for tile in members[k]])
    middle = join_front(before, core0)
    tail = join_back(core1, after)

    seeds = []
    for q in (W0, A01, A012):
        product = weight * total[q]
        gaps = []
        for l in range(2):
            gap = product[l * BATCH : l * BATCH + 1]
            for b in range(1, BATCH):
                gap = gap + product[l * BATCH + b : l * BATCH + b + 1]
            gaps.append(jnp.broadcast_to(gap, (8, 128)))
        seeds.append(2.0 * weight * jnp.where(sub < BATCH, gaps[0], gaps[1]))

    def coefs(ahead, behind):
        tail2 = seeds[1] * behind[W1] + seeds[2] * behind[A12]
        return [seeds[0] + tail2, seeds[1] + seeds[2] * behind[W2], seeds[2], ahead[W0], ahead[A01]]

    of_core0, of_core1 = coefs(before, tail), coefs(middle, after)
    for k in range(5):
        coef_send[k] = of_core1[k] * first + of_core0[k] * (1.0 - first)
        coef[core, k] = of_core0[k] * first + of_core1[k] * (1.0 - first)
    pair_coef = remote(coef_send, coef.at[core], pair_send.at[1], pair_recv.at[1], pair)
    pair_coef.start()

    def slopes(h):
        for l in range(2):
            at = pl.ds(pl.multiple_of(h * HALF + l * 128, 128), 128)
            for b in range(BATCH):
                line = slice(l * BATCH + b, l * BATCH + b + 1)
                c0, c1, s2, e1, e2 = [jnp.broadcast_to(coef[h, k, line, :], (32, 128)) for k in range(5)]
                for t in range(0, STEPS, 32):
                    r = b * STEPS + t
                    here = slice(r, r + 32)

                    def keep(m, value):
                        high, low = halves(value)
                        lanes = slice(m * HALF + l * 128, m * HALF + (l + 1) * 128)
                        sh[h, here, lanes] = high
                        sl[h, here, lanes] = low

                    keep(0, fz[0, here, at] * (c0 + c1 * fb[2, here, at] + s2 * fb[5, here, at]))
                    keep(1, fz[1, here, at] * ((c1 + s2 * fb[3, here, at]) * (e1 + fb[0, here, at])))
                    keep(2, fz[2, here, at] * (s2 * (e2 + e1 * fb[1, here, at] + fb[4, here, at])))

    def increments_part(h):
        wide = dot(sh[h], pt[h])
        return wide[:, 0:CHANS] + wide[:, CHANS : 2 * CHANS] + dot(sl[h], pt[h, :, 0:CHANS])

    def frequencies_part(h, c):
        wide = dot(xt[h, c], sh[h])
        return wide[0:64] + wide[64:128] + dot(xt[h, c, 0:64, :], sl[h])

    upper_rows = (lax.broadcasted_iota(jnp.int32, (8, LEVELS * HALF), 0) < 4).astype(F32)
    ours = upper_rows * first + (1.0 - upper_rows) * (1.0 - first) > 0.5

    def put_frequencies(slot, part, out):
        for j in range(CHIPS // 2):
            mine_rows, rest = gp_half[slot, 8 * j : 8 * (j + 1)], part[8 * j : 8 * (j + 1)]
            out[2 * j] = jnp.where(ours, mine_rows, rest)
            out[2 * j + 1] = jnp.where(ours, rest, mine_rows)

    slopes(core)
    gp_half[0] = frequencies_part(core, other)
    gp_half[1] = frequencies_part(core, core)
    gi_own = increments_part(core)
    for b in range(BATCH):
        gi[b] = gi_own[b * STEPS : (b + 1) * STEPS]
    pair_coef.wait_recv()
    slopes(other)

    put_frequencies(0, frequencies_part(other, other), gp_pair)
    pair_copies = []
    for d in CHIP_ORDER + [0]:
        k = chip_at(d)
        copy = remote(gp_pair.at[k], gp_in.at[k], g_send.at[k], g_recv.at[k], pair)
        copy.start()
        pair_copies.append(copy)
    put_frequencies(1, frequencies_part(other, core), gp_own)
    gi_other = increments_part(other)
    for b in range(BATCH):
        gi[b] = gi[b] + gi_other[b * STEPS : (b + 1) * STEPS]
    z_copies = []
    for d in Z_ORDER:
        k = z_at(d)
        src = gi.at[:, pl.ds(pl.multiple_of(k * PART, PART), PART), :]
        copy = remote(src, gi_in.at[z], z_send.at[k], z_recv.at[z], (tm, k))
        copy.start()
        z_copies.append(copy)
    gp_copies = []
    for d, arrived in zip(CHIP_ORDER, pair_copies):
        k = chip_at(d)
        arrived.wait_recv()
        gp_own[k] = gp_own[k] + gp_in[k]
        copy = remote(gp_own.at[k], gp_recv.at[chip], u_send.at[k], u_recv.at[chip], (2 * k + core, z))
        copy.start()
        gp_copies.append(copy)
    pair_copies[-1].wait_recv()
    gp_recv[chip] = gp_own[chip] + gp_in[chip]
    gi_in[z] = gi[:, pl.ds(pl.multiple_of(z * PART, PART), PART), :]

    for d in Z_ORDER:
        k = z_at(d)
        remote(gi_in.at[k], gi_in.at[k], z_send.at[k], z_recv.at[k], (tm, k)).wait_recv()
    for i in range(2):
        total = gi_in[4 * i]
        for k in range(4 * i + 1, 4 * (i + 1)):
            total = total + gi_in[k]
        for b in range(BATCH):
            gi_out[i, pl.ds(b, PART, stride=BATCH), :] = total[b]

    for d in CHIP_ORDER[::-1]:
        k = chip_at(d)
        remote(gp_recv.at[k], gp_recv.at[k], u_send.at[k], u_recv.at[k], (2 * k + core, z)).wait_recv()
    swap = lax.rem(chip, 2)
    for i in range(2):
        total = gp_recv[8 * i]
        for k in range(8 * i + 1, 8 * (i + 1)):
            total = total + gp_recv[k]
        for m in range(LEVELS):
            lanes = slice(m * HALF, (m + 1) * HALF)
            gp_out[i, m, :, pl.ds(pl.multiple_of(swap * HALF, HALF), HALF)] = total[0:4, lanes]
            gp_out[i, m, :, pl.ds(pl.multiple_of((1 - swap) * HALF, HALF), HALF)] = total[4:8, lanes]
    for copy in [pair_summ, pair_coef] + pair_copies + chip_copies + z_copies + gp_copies:
        copy.wait_send()


def on_device(increments, projections, phases, groups):
    hbm = pl.BlockSpec(memory_space=pltpu.HBM)
    dma = pltpu.SemaphoreType.DMA
    tile = (6, 8, 128)
    wide = LEVELS * HALF
    gi, gp = pl.pallas_call(
        kernel,
        out_shape=(
            pltpu.VMEM((2, PART * BATCH, CHANS), F32),
            pltpu.VMEM((2, LEVELS, CHANS // CHIPS // 2, WIDTH), F32),
        ),
        in_specs=[hbm] * 4,
        out_specs=(pl.BlockSpec(memory_space=pltpu.VMEM),) * 2,
        scratch_shapes=[
            pltpu.VMEM((ROWS, CHANS), F32),
            pltpu.VMEM((LEVELS, CHANS, WIDTH), F32),
            pltpu.VMEM((LEVELS, WIDTH), F32),
            pltpu.SMEM((BATCH,), jnp.int32),
            pltpu.VMEM((ROWS, 6 * CHANS), BF16),
            pltpu.VMEM((2, 2, CHANS, ROWS), BF16),
            pltpu.VMEM((LEVELS, 6 * CHANS, WIDTH), BF16),
            pltpu.VMEM((2, wide, 2 * CHANS), BF16),
            pltpu.VMEM((LEVELS, ROWS, WIDTH), F32),
            pltpu.VMEM((ROWS, WIDTH), F32),
            pltpu.VMEM((LEVELS, 2 * ROWS, WIDTH), BF16),
            pltpu.VMEM((6, ROWS, WIDTH), F32),
            pltpu.VMEM((2, ROWS, wide), BF16),
            pltpu.VMEM((2, ROWS, wide), BF16),
            pltpu.VMEM((2 * STEPS, 2 * STEPS), BF16),
            pltpu.VMEM((2, *tile), F32),
            pltpu.VMEM(tile, F32),
            pltpu.VMEM((CHIPS, *tile), F32),
            pltpu.VMEM((2, 5, 8, 128), F32),
            pltpu.VMEM((5, 8, 128), F32),
            pltpu.VMEM((2, 64, wide), F32),
            pltpu.VMEM((CHIPS, 8, wide), F32),
            pltpu.VMEM((CHIPS, 8, wide), F32),
            pltpu.VMEM((CHIPS, 8, wide), F32),
            pltpu.VMEM((CHIPS, 8, wide), F32),
            pltpu.VMEM((BATCH, STEPS, CHANS), F32),
            pltpu.VMEM((NZ, BATCH, PART, CHANS), F32),
            dma((6,)),
            dma((2,)), dma((2,)),
            dma((CHIPS,)), dma((CHIPS,)),
            dma((CHIPS,)), dma((CHIPS,)),
            dma((CHIPS,)), dma((CHIPS,)),
            dma((NZ,)), dma((NZ,)),
        ],
        compiler_params=pltpu.CompilerParams(
            collective_id=0, has_side_effects=True, vmem_limit_bytes=60 << 20
        ),
    )(
        increments.reshape(ROWS, CHANS),
        projections.transpose(1, 0, 2),
        phases,
        groups,
    )
    return (gi[0] + gi[1]).reshape(PART, BATCH, CHANS), (gp[0] + gp[1]).transpose(1, 0, 2)


def solution(mesh):
    placed = (P("tm", None, None), P(None, None, "freq"), P(None, "freq"), P())
    return jax.shard_map(
        on_device,
        mesh=mesh,
        in_specs=placed,
        out_specs=(P(("tm", "freq"), None, None), P("tm", None, "freq")),
        check_vma=False,
    )
```

```python
import functools
import math

import jax
import jax.numpy as jnp
from jax import lax
from jax.experimental import pallas as pl
from jax.experimental.pallas import tpu as pltpu
from jax.sharding import PartitionSpec as P

MESH = pl.DeviceIdType.MESH
F32 = jnp.float32
BF16 = jnp.bfloat16
TURN = 1.0 / (2.0 * math.pi)

SIN_POLY = (3.14159264, -5.16771008, 2.55007752, -0.59829129, 0.07765766)
COS_POLY = (1.0, -4.93480214, 4.05870916, -1.335212, 0.23493731, -0.02439632)

NY, NX, NZ = 4, 4, 8
CHIPS = NY * NX
STEPS, BATCH, CHANS, WIDTH = 128, 4, 128, 512
LENGTH = STEPS * CHIPS * 2
HALF = WIDTH // 2
ROWS = STEPS * BATCH
PART = STEPS // NZ
LEVELS = 3


def ring(d, count):
    return min(d, count - d)


CHIP_ORDER = sorted(range(1, CHIPS), key=lambda d: -ring(d // NX, NY) - ring(d % NX, NX))
Z_ORDER = sorted(range(1, NZ), key=lambda d: -ring(d, NZ))

W0, W1, W2, A01, A12, A012 = range(6)


def halves(value):
    high = value.astype(BF16)
    return high, (value - high.astype(F32)).astype(BF16)


def dot(left, right):
    return jnp.dot(left, right, preferred_element_type=F32)


def dot_nt(left, right):
    return lax.dot_general(left, right, (((1,), (1,)), ((), ())), preferred_element_type=F32)


def poly(coefs, z):
    value = coefs[-1] * z + coefs[-2]
    for coef in coefs[-3::-1]:
        value = value * z + coef
    return value


def join(early, late):
    return [
        early[W0] + late[W0],
        early[W1] + late[W1],
        early[W2] + late[W2],
        early[A01] + late[A01] + early[W0] * late[W1],
        early[A12] + late[A12] + early[W1] * late[W2],
        early[A012] + late[A012] + early[A01] * late[W2] + early[W0] * late[A12],
    ]


def join_front(early, late):
    return {W0: early[W0] + late[W0], A01: early[A01] + late[A01] + early[W0] * late[W1]}


def join_back(early, late):
    return {
        W1: early[W1] + late[W1],
        W2: early[W2] + late[W2],
        A12: early[A12] + late[A12] + early[W1] * late[W2],
    }


def flag(condition):
    return jnp.where(condition, 1.0, 0.0).astype(F32)


def kernel(
    inc_hbm, proj_hbm, phase_hbm, group_hbm, gi_out, gp_out,
    inc_ref, proj_ref, phase_ref, group_ref, xl, xt, pr, pt, fz, wb, whl, fb, sh, sl, tri,
    summ, summ_in, chips, coef, coef_send, gp_half, gp_pair, gp_own, gp_in, gp_recv, gi, gi_in,
    in_sem, pair_send, pair_recv, g_send, g_recv, c_send, c_recv, u_send, u_recv, z_send, z_recv,
):
    amplitude = math.sqrt(2.0 / LENGTH)
    root = math.sqrt(2.0 * amplitude)
    sin_poly = [root * a for a in SIN_POLY]
    cos_poly = [-root * a for a in COS_POLY]

    loads = [pltpu.make_async_copy(inc_hbm, inc_ref, in_sem.at[0])]
    loads += [pltpu.make_async_copy(proj_hbm.at[m], proj_ref.at[m], in_sem.at[1 + m]) for m in range(LEVELS)]
    loads.append(pltpu.make_async_copy(phase_hbm, phase_ref, in_sem.at[4]))
    loads.append(pltpu.make_async_copy(group_hbm, group_ref, in_sem.at[5]))
    for load in loads:
        load.start()

    tm, z = lax.axis_index("tm"), lax.axis_index("freq")
    core, chip = lax.rem(tm, 2), tm // 2
    other = 1 - core
    pair = (tm + 1 - 2 * core, z)

    def chip_at(d):
        return lax.rem(chip // NX + d // NX, NY) * NX + lax.rem(lax.rem(chip, NX) + d % NX, NX)

    def z_at(d):
        return lax.rem(z + d, NZ)

    barrier = pltpu.get_barrier_semaphore()
    peers = [pair] + [(2 * chip_at(d) + core, z) for d in CHIP_ORDER] + [(tm, z_at(d)) for d in range(1, NZ)]
    for peer in peers:
        pl.semaphore_signal(barrier, inc=1, device_id=peer, device_id_type=MESH)

    def remote(src, dst, send, recv, peer):
        return pltpu.make_async_remote_copy(
            src_ref=src, dst_ref=dst, send_sem=send, recv_sem=recv, device_id=peer, device_id_type=MESH
        )

    row = lax.broadcasted_iota(jnp.int32, (STEPS, STEPS), 0)
    col = lax.broadcasted_iota(jnp.int32, (STEPS, STEPS), 1)
    lower = jnp.where(col < row, 1.0, 0.0).astype(BF16)
    upper = jnp.where(col > row, 1.0, 0.0).astype(BF16)
    for k in range(2):
        tri[0:STEPS, k * STEPS : (k + 1) * STEPS] = lower
        tri[STEPS : 2 * STEPS, k * STEPS : (k + 1) * STEPS] = upper

    loads[0].wait()
    for b in range(BATCH):
        block = inc_ref[pl.ds(b, STEPS, stride=BATCH), :]
        x1 = block.astype(BF16)
        left = block - x1.astype(F32)
        x2 = left.astype(BF16)
        x3 = (left - x2.astype(F32)).astype(BF16)
        at = slice(b * STEPS, (b + 1) * STEPS)
        for k, piece in enumerate((x1, x2, x1, x2, x3, x1)):
            xl[at, k * CHANS : (k + 1) * CHANS] = piece

    for m in range(LEVELS):
        loads[1 + m].wait()

        def split_projection(i, carry, m=m):
            at = pl.ds(pl.multiple_of(i * HALF, HALF), HALF)
            block = proj_ref[m, :, at] * TURN
            p1 = block.astype(BF16)
            left = block - p1.astype(F32)
            p2 = left.astype(BF16)
            p3 = (left - p2.astype(F32)).astype(BF16)
            for k, piece in enumerate((p1, p1, p2, p2, p1, p3)):
                pr[m, k * CHANS : (k + 1) * CHANS, at] = piece
            return carry

        lax.fori_loop(0, 2, split_projection, 0)

    loads[4].wait()
    loads[5].wait()

    pair_summ = remote(summ.at[other], summ_in, pair_send.at[0], pair_recv.at[0], pair)

    def local_sums(i, carry):
        h = lax.rem(core + 1 + i, 2)
        at = pl.ds(pl.multiple_of(h * HALF, HALF), HALF)

        def put(q, b, total):
            for l in range(2):
                summ[h, q, l * BATCH + b : l * BATCH + b + 1, :] = total[:, l * 128 : (l + 1) * 128]

        for m in range(LEVELS):
            turns_all = dot(xl[...], pr[m, :, at])
            shift = phase_ref[m : m + 1, at] * TURN
            for b in range(BATCH):
                total = jnp.zeros((16, HALF), F32)
                for t in range(0, STEPS, 16):
                    r = b * STEPS + t
                    turns = turns_all[r : r + 16] + shift
                    f = turns - jnp.round(turns)
                    fz[m, r : r + 16, at] = f
                    s = f * poly(sin_poly, f * f)
                    w = amplitude - s * s
                    total = total + w
                    if m == 1:
                        wb[r : r + 16, at] = w
                    high, low = halves(w)
                    whl[m, 2 * b * STEPS + t : 2 * b * STEPS + t + 16, at] = high
                    whl[m, (2 * b + 1) * STEPS + t : (2 * b + 1) * STEPS + t + 16, at] = low
                put(m, b, jnp.sum(total, axis=0, keepdims=True))
        for b in range(BATCH):
            here = slice(b * STEPS, (b + 1) * STEPS)
            both = slice(2 * b * STEPS, 2 * (b + 1) * STEPS)
            b0 = dot(tri[0:STEPS, :], whl[0, both, at])
            a2 = dot(tri[STEPS : 2 * STEPS, :], whl[2, both, at])
            fb[0, here, at] = b0
            fb[3, here, at] = a2
            sums = [jnp.zeros((16, HALF), F32)] * 3
            for t in range(0, STEPS, 16):
                w1 = wb[b * STEPS + t : b * STEPS + t + 16, at]
                p, a = b0[t : t + 16] * w1, a2[t : t + 16]
                sums = [sums[0] + p, sums[1] + a * w1, sums[2] + a * p]
            for q, total in zip((A01, A12, A012), sums):
                put(q, b, jnp.sum(total, axis=0, keepdims=True))

        @pl.when(i == 0)
        def _():
            pl.semaphore_wait(barrier, len(peers))
            pair_summ.start()

        return carry

    lax.fori_loop(0, 2, local_sums, 0)

    pair_summ.wait_recv()
    mine = [summ[core, q] for q in range(6)]
    theirs = [summ_in[q] for q in range(6)]
    first = flag(core == 0)
    core0 = [a * first + b * (1.0 - first) for a, b in zip(mine, theirs)]
    core1 = [b * first + a * (1.0 - first) for a, b in zip(mine, theirs)]
    for q, tile in enumerate(join(core0, core1)):
        chips[chip, q] = tile
    chip_copies = []
    for d in CHIP_ORDER:
        k = chip_at(d)
        copy = remote(chips.at[chip], chips.at[chip], c_send.at[k], c_recv.at[chip], (2 * k + core, z))
        copy.start()
        chip_copies.append(copy)

    def scans(i, carry):
        at = pl.ds(pl.multiple_of(i * HALF, HALF), HALF)
        for b in range(BATCH):
            here = slice(b * STEPS, (b + 1) * STEPS)
            both = dot(tri[...], whl[1, 2 * b * STEPS : 2 * (b + 1) * STEPS, at])
            fb[1, here, at] = both[0:STEPS]
            fb[2, here, at] = both[STEPS : 2 * STEPS]
            w1 = wb[here, at]
            fb[4, here, at] = dot(tri[0:STEPS, :], jnp.concatenate(halves(fb[0, here, at] * w1), axis=0))
            fb[5, here, at] = dot(tri[STEPS : 2 * STEPS, :], jnp.concatenate(halves(fb[3, here, at] * w1), axis=0))
        return carry

    lax.fori_loop(0, 2, scans, 0)

    def sines(i, carry):
        at = pl.ds(pl.multiple_of(i * 16, 16), 16)
        for m in range(LEVELS):
            for l in range(0, WIDTH, HALF):
                f = fz[m, at, l : l + HALF]
                f2 = f * f
                fz[m, at, l : l + HALF] = f * poly(sin_poly, f2) * poly(cos_poly, f2)
        return carry

    lax.fori_loop(0, ROWS // 16, sines, 0)

    for h in range(2):
        for m in range(LEVELS):
            for l in range(2):
                lanes = slice(h * HALF + l * 128, h * HALF + (l + 1) * 128)
                high, low = halves(proj_ref[m, :, lanes].T)
                down = slice(m * HALF + l * 128, m * HALF + (l + 1) * 128)
                pt[h, down, 0:CHANS] = high
                pt[h, down, CHANS : 2 * CHANS] = low

    for order in range(2):
        place = lax.rem(row, 64)
        k = place // 4
        k = k + order * (1 - 2 * lax.rem(k, 2))
        channel = 8 * k + 4 * (row // 64) + lax.rem(place, 4)
        pick = jnp.where(col == channel, 1.0, 0.0).astype(BF16)
        for b in range(BATCH):
            at = slice(b * STEPS, (b + 1) * STEPS)
            high = dot_nt(pick, xl[at, 0:CHANS]).astype(BF16)
            low = dot_nt(pick, xl[at, CHANS : 2 * CHANS]).astype(BF16)
            for c in range(2):
                xt[order, c, 0:64, at] = high[64 * c : 64 * (c + 1)]
                xt[order, c, 64:128, at] = low[64 * c : 64 * (c + 1)]

    sub = lax.broadcasted_iota(jnp.int32, (8, 128), 0)
    weight = jnp.zeros((8, 128), F32)
    for b in range(BATCH):
        sign = jnp.where(group_ref[b] == 1, 2.0 / BATCH, -2.0 / BATCH).astype(F32)
        weight = jnp.where(lax.rem(sub, BATCH) == b, sign, weight)

    for d in CHIP_ORDER:
        k = chip_at(d)
        remote(chips.at[k], chips.at[k], c_send.at[k], c_recv.at[k], (2 * k + core, z)).wait_recv()
    members = [[chips[k, q] for q in range(6)] for k in range(CHIPS)]
    total = members[0]
    for k in range(1, CHIPS):
        total = join(total, members[k])
    zero = jnp.zeros((8, 128), F32)
    before = [zero] * 6
    for k in range(CHIPS - 1):
        keep = flag(chip > k)
        before = join_front(before, [tile * keep for tile in members[k]])
    after = [zero] * 6
    for k in range(1, CHIPS):
        keep = flag(chip < k)
        after = join_back(after, [tile * keep for tile in members[k]])
    middle = join_front(before, core0)
    tail = join_back(core1, after)

    seeds = []
    for q in (W0, A01, A012):
        product = weight * total[q]
        gaps = []
        for l in range(2):
            gap = product[l * BATCH : l * BATCH + 1]
            for b in range(1, BATCH):
                gap = gap + product[l * BATCH + b : l * BATCH + b + 1]
            gaps.append(jnp.broadcast_to(gap, (8, 128)))
        seeds.append(2.0 * weight * jnp.where(sub < BATCH, gaps[0], gaps[1]))

    def coefs(ahead, behind):
        tail2 = seeds[1] * behind[W1] + seeds[2] * behind[A12]
        return [seeds[0] + tail2, seeds[1] + seeds[2] * behind[W2], seeds[2], ahead[W0], ahead[A01]]

    of_core0, of_core1 = coefs(before, tail), coefs(middle, after)
    for k in range(5):
        coef_send[k] = of_core1[k] * first + of_core0[k] * (1.0 - first)
        coef[core, k] = of_core0[k] * first + of_core1[k] * (1.0 - first)
    pair_coef = remote(coef_send, coef.at[core], pair_send.at[1], pair_recv.at[1], pair)
    pair_coef.start()

    def slopes(h):
        for l in range(2):
            at = pl.ds(pl.multiple_of(h * HALF + l * 128, 128), 128)
            for b in range(BATCH):
                line = slice(l * BATCH + b, l * BATCH + b + 1)
                c0, c1, s2, e1, e2 = [jnp.broadcast_to(coef[h, k, line, :], (32, 128)) for k in range(5)]
                for t in range(0, STEPS, 32):
                    r = b * STEPS + t
                    here = slice(r, r + 32)

                    def keep(m, value):
                        high, low = halves(value)
                        lanes = slice(m * HALF + l * 128, m * HALF + (l + 1) * 128)
                        sh[h, here, lanes] = high
                        sl[h, here, lanes] = low

                    keep(0, fz[0, here, at] * (c0 + c1 * fb[2, here, at] + s2 * fb[5, here, at]))
                    keep(1, fz[1, here, at] * ((c1 + s2 * fb[3, here, at]) * (e1 + fb[0, here, at])))
                    keep(2, fz[2, here, at] * (s2 * (e2 + e1 * fb[1, here, at] + fb[4, here, at])))

    def increments_part(h):
        wide = dot(sh[h], pt[h])
        return wide[:, 0:CHANS] + wide[:, CHANS : 2 * CHANS] + dot(sl[h], pt[h, :, 0:CHANS])

    def frequencies_part(h, c):
        wide = dot(xt[h, c], sh[h])
        return wide[0:64] + wide[64:128] + dot(xt[h, c, 0:64, :], sl[h])

    upper_rows = (lax.broadcasted_iota(jnp.int32, (8, LEVELS * HALF), 0) < 4).astype(F32)
    ours = upper_rows * first + (1.0 - upper_rows) * (1.0 - first) > 0.5

    def put_frequencies(slot, part, out):
        for j in range(CHIPS // 2):
            mine_rows, rest = gp_half[slot, 8 * j : 8 * (j + 1)], part[8 * j : 8 * (j + 1)]
            out[2 * j] = jnp.where(ours, mine_rows, rest)
            out[2 * j + 1] = jnp.where(ours, rest, mine_rows)

    slopes(core)
    gp_half[0] = frequencies_part(core, other)
    gp_half[1] = frequencies_part(core, core)
    gi_own = increments_part(core)
    for b in range(BATCH):
        gi[b] = gi_own[b * STEPS : (b + 1) * STEPS]
    pair_coef.wait_recv()
    slopes(other)

    put_frequencies(0, frequencies_part(other, other), gp_pair)
    pair_copies = []
    for d in CHIP_ORDER + [0]:
        k = chip_at(d)
        copy = remote(gp_pair.at[k], gp_in.at[k], g_send.at[k], g_recv.at[k], pair)
        copy.start()
        pair_copies.append(copy)
    gi_other = increments_part(other)
    for b in range(BATCH):
        gi[b] = gi[b] + gi_other[b * STEPS : (b + 1) * STEPS]
    z_copies = []
    for d in Z_ORDER:
        k = z_at(d)
        src = gi.at[:, pl.ds(pl.multiple_of(k * PART, PART), PART), :]
        copy = remote(src, gi_in.at[z], z_send.at[k], z_recv.at[z], (tm, k))
        copy.start()
        z_copies.append(copy)
    put_frequencies(1, frequencies_part(other, core), gp_own)
    gp_copies = []
    for d, arrived in zip(CHIP_ORDER, pair_copies):
        k = chip_at(d)
        arrived.wait_recv()
        gp_own[k] = gp_own[k] + gp_in[k]
        copy = remote(gp_own.at[k], gp_recv.at[chip], u_send.at[k], u_recv.at[chip], (2 * k + core, z))
        copy.start()
        gp_copies.append(copy)
    pair_copies[-1].wait_recv()
    gp_recv[chip] = gp_own[chip] + gp_in[chip]
    gi_in[z] = gi[:, pl.ds(pl.multiple_of(z * PART, PART), PART), :]

    for d in Z_ORDER:
        k = z_at(d)
        remote(gi_in.at[k], gi_in.at[k], z_send.at[k], z_recv.at[k], (tm, k)).wait_recv()
    total = gi_in[0]
    for k in range(1, NZ):
        total = total + gi_in[k]
    for b in range(BATCH):
        gi_out[pl.ds(b, PART, stride=BATCH), :] = total[b]

    for d in CHIP_ORDER[::-1]:
        k = chip_at(d)
        remote(gp_recv.at[k], gp_recv.at[k], u_send.at[k], u_recv.at[k], (2 * k + core, z)).wait_recv()
    swap = lax.rem(chip, 2)
    total = gp_recv[0]
    for k in range(1, CHIPS):
        total = total + gp_recv[k]
    for m in range(LEVELS):
        lanes = slice(m * HALF, (m + 1) * HALF)
        gp_out[m, :, pl.ds(pl.multiple_of(swap * HALF, HALF), HALF)] = total[0:4, lanes]
        gp_out[m, :, pl.ds(pl.multiple_of((1 - swap) * HALF, HALF), HALF)] = total[4:8, lanes]
    for copy in [pair_summ, pair_coef] + pair_copies + chip_copies + z_copies + gp_copies:
        copy.wait_send()


def store(gi_ref, gp_ref, gi_hbm, gp_hbm, sem):
    copies = [
        pltpu.make_async_copy(gi_ref, gi_hbm, sem.at[0]),
        pltpu.make_async_copy(gp_ref, gp_hbm, sem.at[1]),
    ]
    for copy in copies:
        copy.start()
    for copy in copies:
        copy.wait()


def on_device(increments, projections, phases, groups):
    hbm = pl.BlockSpec(memory_space=pltpu.HBM)
    dma = pltpu.SemaphoreType.DMA
    tile = (6, 8, 128)
    wide = LEVELS * HALF
    gi_shape, gp_shape = (PART * BATCH, CHANS), (LEVELS, CHANS // CHIPS // 2, WIDTH)
    vmem = pl.BlockSpec(memory_space=pltpu.VMEM)
    gi, gp = pl.pallas_call(
        kernel,
        out_shape=(
            pltpu.VMEM(gi_shape, F32),
            pltpu.VMEM(gp_shape, F32),
        ),
        in_specs=[hbm] * 4,
        out_specs=(vmem, vmem),
        scratch_shapes=[
            pltpu.VMEM((ROWS, CHANS), F32),
            pltpu.VMEM((LEVELS, CHANS, WIDTH), F32),
            pltpu.VMEM((LEVELS, WIDTH), F32),
            pltpu.SMEM((BATCH,), jnp.int32),
            pltpu.VMEM((ROWS, 6 * CHANS), BF16),
            pltpu.VMEM((2, 2, CHANS, ROWS), BF16),
            pltpu.VMEM((LEVELS, 6 * CHANS, WIDTH), BF16),
            pltpu.VMEM((2, wide, 2 * CHANS), BF16),
            pltpu.VMEM((LEVELS, ROWS, WIDTH), F32),
            pltpu.VMEM((ROWS, WIDTH), F32),
            pltpu.VMEM((LEVELS, 2 * ROWS, WIDTH), BF16),
            pltpu.VMEM((6, ROWS, WIDTH), F32),
            pltpu.VMEM((2, ROWS, wide), BF16),
            pltpu.VMEM((2, ROWS, wide), BF16),
            pltpu.VMEM((2 * STEPS, 2 * STEPS), BF16),
            pltpu.VMEM((2, *tile), F32),
            pltpu.VMEM(tile, F32),
            pltpu.VMEM((CHIPS, *tile), F32),
            pltpu.VMEM((2, 5, 8, 128), F32),
            pltpu.VMEM((5, 8, 128), F32),
            pltpu.VMEM((2, 64, wide), F32),
            pltpu.VMEM((CHIPS, 8, wide), F32),
            pltpu.VMEM((CHIPS, 8, wide), F32),
            pltpu.VMEM((CHIPS, 8, wide), F32),
            pltpu.VMEM((CHIPS, 8, wide), F32),
            pltpu.VMEM((BATCH, STEPS, CHANS), F32),
            pltpu.VMEM((NZ, BATCH, PART, CHANS), F32),
            dma((6,)),
            dma((2,)), dma((2,)),
            dma((CHIPS,)), dma((CHIPS,)),
            dma((CHIPS,)), dma((CHIPS,)),
            dma((CHIPS,)), dma((CHIPS,)),
            dma((NZ,)), dma((NZ,)),
        ],
        compiler_params=pltpu.CompilerParams(
            collective_id=0, has_side_effects=True, vmem_limit_bytes=60 << 20
        ),
    )(
        increments.reshape(ROWS, CHANS),
        projections.transpose(1, 0, 2),
        phases,
        groups,
    )
    gi, gp = pl.pallas_call(
        store,
        out_shape=(jax.ShapeDtypeStruct(gi_shape, F32), jax.ShapeDtypeStruct(gp_shape, F32)),
        in_specs=[vmem, vmem],
        out_specs=(hbm, hbm),
        scratch_shapes=[dma((2,))],
        compiler_params=pltpu.CompilerParams(vmem_limit_bytes=1 << 20),
    )(gi, gp)
    return gi.reshape(PART, BATCH, CHANS), gp.transpose(1, 0, 2)


def solution(mesh):
    placed = (P("tm", None, None), P(None, None, "freq"), P(None, "freq"), P())
    return jax.shard_map(
        on_device,
        mesh=mesh,
        in_specs=placed,
        out_specs=(P(("tm", "freq"), None, None), P("tm", None, "freq")),
        check_vma=False,
    )
```

```python
import functools
import math

import jax
import jax.numpy as jnp
from jax import lax
from jax.experimental import pallas as pl
from jax.experimental.pallas import tpu as pltpu
from jax.sharding import PartitionSpec as P

MESH = pl.DeviceIdType.MESH
F32 = jnp.float32
BF16 = jnp.bfloat16
TURN = 1.0 / (2.0 * math.pi)

SIN_POLY = (3.14159264, -5.16771008, 2.55007752, -0.59829129, 0.07765766)
COS_POLY = (1.0, -4.93480214, 4.05870916, -1.335212, 0.23493731, -0.02439632)

NY, NX, NZ = 4, 4, 8
CHIPS = NY * NX
STEPS, BATCH, CHANS, WIDTH = 128, 4, 128, 512
LENGTH = STEPS * CHIPS * 2
HALF = WIDTH // 2
ROWS = STEPS * BATCH
PART = STEPS // NZ
LEVELS = 3


def ring(d, count):
    return min(d, count - d)


CHIP_ORDER = sorted(range(1, CHIPS), key=lambda d: -ring(d // NX, NY) - ring(d % NX, NX))
Z_ORDER = sorted(range(1, NZ), key=lambda d: -ring(d, NZ))

W0, W1, W2, A01, A12, A012 = range(6)


def halves(value):
    high = value.astype(BF16)
    return high, (value - high.astype(F32)).astype(BF16)


def dot(left, right):
    return jnp.dot(left, right, preferred_element_type=F32)


def dot_nt(left, right):
    return lax.dot_general(left, right, (((1,), (1,)), ((), ())), preferred_element_type=F32)


def poly(coefs, z):
    value = coefs[-1] * z + coefs[-2]
    for coef in coefs[-3::-1]:
        value = value * z + coef
    return value


def join(early, late):
    return [
        early[W0] + late[W0],
        early[W1] + late[W1],
        early[W2] + late[W2],
        early[A01] + late[A01] + early[W0] * late[W1],
        early[A12] + late[A12] + early[W1] * late[W2],
        early[A012] + late[A012] + early[A01] * late[W2] + early[W0] * late[A12],
    ]


def join_front(early, late):
    return {W0: early[W0] + late[W0], A01: early[A01] + late[A01] + early[W0] * late[W1]}


def join_back(early, late):
    return {
        W1: early[W1] + late[W1],
        W2: early[W2] + late[W2],
        A12: early[A12] + late[A12] + early[W1] * late[W2],
    }


def flag(condition):
    return jnp.where(condition, 1.0, 0.0).astype(F32)


def kernel(
    inc_hbm, proj_hbm, phase_hbm, group_hbm, gi_out, gp_out,
    inc_ref, proj_ref, phase_ref, group_ref, xl, xt, pr, pt, fz, wb, whl, fb, sh, sl, tri,
    summ, summ_in, chips, coef, coef_send, gp_half, gp_pair, gp_own, gp_in, gp_recv, gi, gi_in,
    in_sem, pair_send, pair_recv, g_send, g_recv, c_send, c_recv, u_send, u_recv, z_send, z_recv,
):
    amplitude = math.sqrt(2.0 / LENGTH)
    root = math.sqrt(2.0 * amplitude)
    sin_poly = [root * a for a in SIN_POLY]
    cos_poly = [-root * a for a in COS_POLY]

    loads = [pltpu.make_async_copy(inc_hbm, inc_ref, in_sem.at[0])]
    loads += [pltpu.make_async_copy(proj_hbm.at[m], proj_ref.at[m], in_sem.at[1 + m]) for m in range(LEVELS)]
    loads.append(pltpu.make_async_copy(phase_hbm, phase_ref, in_sem.at[4]))
    loads.append(pltpu.make_async_copy(group_hbm, group_ref, in_sem.at[5]))
    for load in loads:
        load.start()

    tm, z = lax.axis_index("tm"), lax.axis_index("freq")
    core, chip = lax.rem(tm, 2), tm // 2
    other = 1 - core
    pair = (tm + 1 - 2 * core, z)

    def chip_at(d):
        return lax.rem(chip // NX + d // NX, NY) * NX + lax.rem(lax.rem(chip, NX) + d % NX, NX)

    def z_at(d):
        return lax.rem(z + d, NZ)

    barrier = pltpu.get_barrier_semaphore()
    peers = [pair] + [(2 * chip_at(d) + core, z) for d in CHIP_ORDER] + [(tm, z_at(d)) for d in range(1, NZ)]
    for peer in peers:
        pl.semaphore_signal(barrier, inc=1, device_id=peer, device_id_type=MESH)

    def remote(src, dst, send, recv, peer):
        return pltpu.make_async_remote_copy(
            src_ref=src, dst_ref=dst, send_sem=send, recv_sem=recv, device_id=peer, device_id_type=MESH
        )

    row = lax.broadcasted_iota(jnp.int32, (STEPS, STEPS), 0)
    col = lax.broadcasted_iota(jnp.int32, (STEPS, STEPS), 1)
    lower = jnp.where(col < row, 1.0, 0.0).astype(BF16)
    upper = jnp.where(col > row, 1.0, 0.0).astype(BF16)
    for k in range(2):
        tri[0:STEPS, k * STEPS : (k + 1) * STEPS] = lower
        tri[STEPS : 2 * STEPS, k * STEPS : (k + 1) * STEPS] = upper

    loads[0].wait()
    for b in range(BATCH):
        block = inc_ref[pl.ds(b, STEPS, stride=BATCH), :]
        x1 = block.astype(BF16)
        left = block - x1.astype(F32)
        x2 = left.astype(BF16)
        x3 = (left - x2.astype(F32)).astype(BF16)
        at = slice(b * STEPS, (b + 1) * STEPS)
        for k, piece in enumerate((x1, x2, x1, x2, x3, x1)):
            xl[at, k * CHANS : (k + 1) * CHANS] = piece

    for load in loads[1:4]:
        load.wait()

    def split_projection(m, h):
        at = pl.ds(pl.multiple_of(h * HALF, HALF), HALF)
        block = proj_ref[m, :, at] * TURN
        p1 = block.astype(BF16)
        left = block - p1.astype(F32)
        p2 = left.astype(BF16)
        p3 = (left - p2.astype(F32)).astype(BF16)
        for k, piece in enumerate((p1, p1, p2, p2, p1, p3)):
            pr[m, k * CHANS : (k + 1) * CHANS, at] = piece

    loads[4].wait()
    loads[5].wait()

    pair_summ = remote(summ.at[other], summ_in, pair_send.at[0], pair_recv.at[0], pair)

    def put(h, q, b, total):
        for l in range(2):
            summ[h, q, l * BATCH + b : l * BATCH + b + 1, :] = total[:, l * 128 : (l + 1) * 128]

    def columns(h):
        return pl.ds(pl.multiple_of(h * HALF, HALF), HALF)

    def angles(m, h):
        return dot(xl[...], pr[m, :, columns(h)])

    def waves(m, h, turns_all):
        at = columns(h)
        shift = phase_ref[m : m + 1, at] * TURN
        for b in range(BATCH):
            total = jnp.zeros((16, HALF), F32)
            for t in range(0, STEPS, 16):
                r = b * STEPS + t
                turns = turns_all[r : r + 16] + shift
                f = turns - jnp.round(turns)
                fz[m, r : r + 16, at] = f
                s = f * poly(sin_poly, f * f)
                w = amplitude - s * s
                total = total + w
                if m == 1:
                    wb[r : r + 16, at] = w
                else:
                    high, low = halves(w)
                    whl[m // 2, 2 * b * STEPS + t : 2 * b * STEPS + t + 16, at] = high
                    whl[m // 2, (2 * b + 1) * STEPS + t : (2 * b + 1) * STEPS + t + 16, at] = low
            put(h, m, b, jnp.sum(total, axis=0, keepdims=True))

    def local_scan(h, slot, level, row0):
        at = columns(h)
        for b in range(BATCH):
            both = slice(2 * b * STEPS, 2 * (b + 1) * STEPS)
            fb[slot, b * STEPS : (b + 1) * STEPS, at] = dot(tri[row0 : row0 + STEPS, :], whl[level, both, at])

    def local_sums(h):
        at = columns(h)
        for b in range(BATCH):
            sums = [jnp.zeros((16, HALF), F32)] * 3
            for t in range(0, STEPS, 16):
                r = b * STEPS + t
                w1, a = wb[r : r + 16, at], fb[3, r : r + 16, at]
                p = fb[0, r : r + 16, at] * w1
                sums = [sums[0] + p, sums[1] + a * w1, sums[2] + a * p]
            for q, total in zip((A01, A12, A012), sums):
                put(h, q, b, jnp.sum(total, axis=0, keepdims=True))

    def half_sums(i, carry):
        h = lax.rem(core + 1 + i, 2)
        split_projection(0, h)
        turns = angles(0, h)
        split_projection(2, h)
        later = angles(2, h)
        split_projection(1, h)
        waves(0, h, turns)
        turns = angles(1, h)
        waves(2, h, later)
        local_scan(h, 0, 0, 0)
        local_scan(h, 3, 1, STEPS)
        waves(1, h, turns)
        local_sums(h)

        @pl.when(i == 0)
        def _():
            pl.semaphore_wait(barrier, len(peers))
            pair_summ.start()

        return carry

    lax.fori_loop(0, 2, half_sums, 0)

    pair_summ.wait_recv()
    mine = [summ[core, q] for q in range(6)]
    theirs = [summ_in[q] for q in range(6)]
    first = flag(core == 0)
    core0 = [a * first + b * (1.0 - first) for a, b in zip(mine, theirs)]
    core1 = [b * first + a * (1.0 - first) for a, b in zip(mine, theirs)]
    for q, tile in enumerate(join(core0, core1)):
        chips[chip, q] = tile
    chip_copies = []
    for d in CHIP_ORDER:
        k = chip_at(d)
        copy = remote(chips.at[chip], chips.at[chip], c_send.at[k], c_recv.at[chip], (2 * k + core, z))
        copy.start()
        chip_copies.append(copy)

    def scans(i, carry):
        at = pl.ds(pl.multiple_of(i * HALF, HALF), HALF)
        for b in range(BATCH):
            here = slice(b * STEPS, (b + 1) * STEPS)
            w1 = wb[here, at]
            both = dot(tri[...], jnp.concatenate(halves(w1), axis=0))
            fb[1, here, at] = both[0:STEPS]
            fb[2, here, at] = both[STEPS : 2 * STEPS]
            fb[4, here, at] = dot(tri[0:STEPS, :], jnp.concatenate(halves(fb[0, here, at] * w1), axis=0))
            fb[5, here, at] = dot(tri[STEPS : 2 * STEPS, :], jnp.concatenate(halves(fb[3, here, at] * w1), axis=0))
        return carry

    lax.fori_loop(0, 2, scans, 0)

    def sines(i, carry):
        at = pl.ds(pl.multiple_of(i * 16, 16), 16)
        for m in range(LEVELS):
            for l in range(0, WIDTH, HALF):
                f = fz[m, at, l : l + HALF]
                f2 = f * f
                fz[m, at, l : l + HALF] = f * poly(sin_poly, f2) * poly(cos_poly, f2)
        return carry

    lax.fori_loop(0, ROWS // 16, sines, 0)

    for h in range(2):
        for m in range(LEVELS):
            for l in range(2):
                lanes = slice(h * HALF + l * 128, h * HALF + (l + 1) * 128)
                high, low = halves(proj_ref[m, :, lanes].T)
                down = slice(m * HALF + l * 128, m * HALF + (l + 1) * 128)
                pt[h, down, 0:CHANS] = high
                pt[h, down, CHANS : 2 * CHANS] = low

    for order in range(2):
        place = lax.rem(row, 64)
        k = place // 4
        k = k + order * (1 - 2 * lax.rem(k, 2))
        channel = 8 * k + 4 * (row // 64) + lax.rem(place, 4)
        pick = jnp.where(col == channel, 1.0, 0.0).astype(BF16)
        for b in range(BATCH):
            at = slice(b * STEPS, (b + 1) * STEPS)
            high = dot_nt(pick, xl[at, 0:CHANS]).astype(BF16)
            low = dot_nt(pick, xl[at, CHANS : 2 * CHANS]).astype(BF16)
            for c in range(2):
                xt[order, c, 0:64, at] = high[64 * c : 64 * (c + 1)]
                xt[order, c, 64:128, at] = low[64 * c : 64 * (c + 1)]

    sub = lax.broadcasted_iota(jnp.int32, (8, 128), 0)
    weight = jnp.zeros((8, 128), F32)
    for b in range(BATCH):
        sign = jnp.where(group_ref[b] == 1, 2.0 / BATCH, -2.0 / BATCH).astype(F32)
        weight = jnp.where(lax.rem(sub, BATCH) == b, sign, weight)

    for d in CHIP_ORDER:
        k = chip_at(d)
        remote(chips.at[k], chips.at[k], c_send.at[k], c_recv.at[k], (2 * k + core, z)).wait_recv()
    members = [[chips[k, q] for q in range(6)] for k in range(CHIPS)]
    total = members[0]
    for k in range(1, CHIPS):
        total = join(total, members[k])
    zero = jnp.zeros((8, 128), F32)
    before = [zero] * 6
    for k in range(CHIPS - 1):
        keep = flag(chip > k)
        before = join_front(before, [tile * keep for tile in members[k]])
    after = [zero] * 6
    for k in range(1, CHIPS):
        keep = flag(chip < k)
        after = join_back(after, [tile * keep for tile in members[k]])
    middle = join_front(before, core0)
    tail = join_back(core1, after)

    seeds = []
    for q in (W0, A01, A012):
        product = weight * total[q]
        gaps = []
        for l in range(2):
            gap = product[l * BATCH : l * BATCH + 1]
            for b in range(1, BATCH):
                gap = gap + product[l * BATCH + b : l * BATCH + b + 1]
            gaps.append(jnp.broadcast_to(gap, (8, 128)))
        seeds.append(2.0 * weight * jnp.where(sub < BATCH, gaps[0], gaps[1]))

    def coefs(ahead, behind):
        tail2 = seeds[1] * behind[W1] + seeds[2] * behind[A12]
        return [seeds[0] + tail2, seeds[1] + seeds[2] * behind[W2], seeds[2], ahead[W0], ahead[A01]]

    of_core0, of_core1 = coefs(before, tail), coefs(middle, after)
    for k in range(5):
        coef_send[k] = of_core1[k] * first + of_core0[k] * (1.0 - first)
        coef[core, k] = of_core0[k] * first + of_core1[k] * (1.0 - first)
    pair_coef = remote(coef_send, coef.at[core], pair_send.at[1], pair_recv.at[1], pair)
    pair_coef.start()

    def slopes(h):
        for l in range(2):
            at = pl.ds(pl.multiple_of(h * HALF + l * 128, 128), 128)
            for b in range(BATCH):
                line = slice(l * BATCH + b, l * BATCH + b + 1)
                c0, c1, s2, e1, e2 = [jnp.broadcast_to(coef[h, k, line, :], (32, 128)) for k in range(5)]
                for t in range(0, STEPS, 32):
                    r = b * STEPS + t
                    here = slice(r, r + 32)

                    def keep(m, value):
                        high, low = halves(value)
                        lanes = slice(m * HALF + l * 128, m * HALF + (l + 1) * 128)
                        sh[h, here, lanes] = high
                        sl[h, here, lanes] = low

                    keep(0, fz[0, here, at] * (c0 + c1 * fb[2, here, at] + s2 * fb[5, here, at]))
                    keep(1, fz[1, here, at] * ((c1 + s2 * fb[3, here, at]) * (e1 + fb[0, here, at])))
                    keep(2, fz[2, here, at] * (s2 * (e2 + e1 * fb[1, here, at] + fb[4, here, at])))

    def increments_part(h):
        wide = dot(sh[h], pt[h])
        return wide[:, 0:CHANS] + wide[:, CHANS : 2 * CHANS] + dot(sl[h], pt[h, :, 0:CHANS])

    def frequencies_part(h, c):
        wide = dot(xt[h, c], sh[h])
        return wide[0:64] + wide[64:128] + dot(xt[h, c, 0:64, :], sl[h])

    upper_rows = (lax.broadcasted_iota(jnp.int32, (8, LEVELS * HALF), 0) < 4).astype(F32)
    ours = upper_rows * first + (1.0 - upper_rows) * (1.0 - first) > 0.5

    def put_frequencies(slot, part, out):
        for j in range(CHIPS // 2):
            mine_rows, rest = gp_half[slot, 8 * j : 8 * (j + 1)], part[8 * j : 8 * (j + 1)]
            out[2 * j] = jnp.where(ours, mine_rows, rest)
            out[2 * j + 1] = jnp.where(ours, rest, mine_rows)

    slopes(core)
    gp_half[0] = frequencies_part(core, other)
    gp_half[1] = frequencies_part(core, core)
    gi_own = increments_part(core)
    for b in range(BATCH):
        gi[b] = gi_own[b * STEPS : (b + 1) * STEPS]
    pair_coef.wait_recv()
    slopes(other)

    put_frequencies(0, frequencies_part(other, other), gp_pair)
    pair_copies = []
    for d in CHIP_ORDER + [0]:
        k = chip_at(d)
        copy = remote(gp_pair.at[k], gp_in.at[k], g_send.at[k], g_recv.at[k], pair)
        copy.start()
        pair_copies.append(copy)
    gi_other = increments_part(other)
    for b in range(BATCH):
        gi[b] = gi[b] + gi_other[b * STEPS : (b + 1) * STEPS]
    z_copies = []
    for d in Z_ORDER:
        k = z_at(d)
        src = gi.at[:, pl.ds(pl.multiple_of(k * PART, PART), PART), :]
        copy = remote(src, gi_in.at[z], z_send.at[k], z_recv.at[z], (tm, k))
        copy.start()
        z_copies.append(copy)
    put_frequencies(1, frequencies_part(other, core), gp_own)
    gp_copies = []
    for d, arrived in zip(CHIP_ORDER, pair_copies):
        k = chip_at(d)
        arrived.wait_recv()
        gp_own[k] = gp_own[k] + gp_in[k]
        copy = remote(gp_own.at[k], gp_recv.at[chip], u_send.at[k], u_recv.at[chip], (2 * k + core, z))
        copy.start()
        gp_copies.append(copy)
    pair_copies[-1].wait_recv()
    gp_recv[chip] = gp_own[chip] + gp_in[chip]
    gi_in[z] = gi[:, pl.ds(pl.multiple_of(z * PART, PART), PART), :]

    for d in Z_ORDER:
        k = z_at(d)
        remote(gi_in.at[k], gi_in.at[k], z_send.at[k], z_recv.at[k], (tm, k)).wait_recv()
    total = gi_in[0]
    for k in range(1, NZ):
        total = total + gi_in[k]
    for b in range(BATCH):
        gi_out[pl.ds(b, PART, stride=BATCH), :] = total[b]

    for d in CHIP_ORDER[::-1]:
        k = chip_at(d)
        remote(gp_recv.at[k], gp_recv.at[k], u_send.at[k], u_recv.at[k], (2 * k + core, z)).wait_recv()
    swap = lax.rem(chip, 2)
    total = gp_recv[0]
    for k in range(1, CHIPS):
        total = total + gp_recv[k]
    for m in range(LEVELS):
        lanes = slice(m * HALF, (m + 1) * HALF)
        gp_out[m, :, pl.ds(pl.multiple_of(swap * HALF, HALF), HALF)] = total[0:4, lanes]
        gp_out[m, :, pl.ds(pl.multiple_of((1 - swap) * HALF, HALF), HALF)] = total[4:8, lanes]
    for copy in [pair_summ, pair_coef] + pair_copies + chip_copies + z_copies + gp_copies:
        copy.wait_send()


def store(gi_ref, gp_ref, gi_hbm, gp_hbm, sem):
    copies = [
        pltpu.make_async_copy(gi_ref, gi_hbm, sem.at[0]),
        pltpu.make_async_copy(gp_ref, gp_hbm, sem.at[1]),
    ]
    for copy in copies:
        copy.start()
    for copy in copies:
        copy.wait()


def on_device(increments, projections, phases, groups):
    hbm = pl.BlockSpec(memory_space=pltpu.HBM)
    dma = pltpu.SemaphoreType.DMA
    tile = (6, 8, 128)
    wide = LEVELS * HALF
    gi_shape, gp_shape = (PART * BATCH, CHANS), (LEVELS, CHANS // CHIPS // 2, WIDTH)
    vmem = pl.BlockSpec(memory_space=pltpu.VMEM)
    gi, gp = pl.pallas_call(
        kernel,
        out_shape=(
            pltpu.VMEM(gi_shape, F32),
            pltpu.VMEM(gp_shape, F32),
        ),
        in_specs=[hbm] * 4,
        out_specs=(vmem, vmem),
        scratch_shapes=[
            pltpu.VMEM((ROWS, CHANS), F32),
            pltpu.VMEM((LEVELS, CHANS, WIDTH), F32),
            pltpu.VMEM((LEVELS, WIDTH), F32),
            pltpu.SMEM((BATCH,), jnp.int32),
            pltpu.VMEM((ROWS, 6 * CHANS), BF16),
            pltpu.VMEM((2, 2, CHANS, ROWS), BF16),
            pltpu.VMEM((LEVELS, 6 * CHANS, WIDTH), BF16),
            pltpu.VMEM((2, wide, 2 * CHANS), BF16),
            pltpu.VMEM((LEVELS, ROWS, WIDTH), F32),
            pltpu.VMEM((ROWS, WIDTH), F32),
            pltpu.VMEM((2, 2 * ROWS, WIDTH), BF16),
            pltpu.VMEM((6, ROWS, WIDTH), F32),
            pltpu.VMEM((2, ROWS, wide), BF16),
            pltpu.VMEM((2, ROWS, wide), BF16),
            pltpu.VMEM((2 * STEPS, 2 * STEPS), BF16),
            pltpu.VMEM((2, *tile), F32),
            pltpu.VMEM(tile, F32),
            pltpu.VMEM((CHIPS, *tile), F32),
            pltpu.VMEM((2, 5, 8, 128), F32),
            pltpu.VMEM((5, 8, 128), F32),
            pltpu.VMEM((2, 64, wide), F32),
            pltpu.VMEM((CHIPS, 8, wide), F32),
            pltpu.VMEM((CHIPS, 8, wide), F32),
            pltpu.VMEM((CHIPS, 8, wide), F32),
            pltpu.VMEM((CHIPS, 8, wide), F32),
            pltpu.VMEM((BATCH, STEPS, CHANS), F32),
            pltpu.VMEM((NZ, BATCH, PART, CHANS), F32),
            dma((6,)),
            dma((2,)), dma((2,)),
            dma((CHIPS,)), dma((CHIPS,)),
            dma((CHIPS,)), dma((CHIPS,)),
            dma((CHIPS,)), dma((CHIPS,)),
            dma((NZ,)), dma((NZ,)),
        ],
        compiler_params=pltpu.CompilerParams(
            collective_id=0, has_side_effects=True, vmem_limit_bytes=60 << 20
        ),
    )(
        increments.reshape(ROWS, CHANS),
        projections.transpose(1, 0, 2),
        phases,
        groups,
    )
    gi, gp = pl.pallas_call(
        store,
        out_shape=(jax.ShapeDtypeStruct(gi_shape, F32), jax.ShapeDtypeStruct(gp_shape, F32)),
        in_specs=[vmem, vmem],
        out_specs=(hbm, hbm),
        scratch_shapes=[dma((2,))],
        compiler_params=pltpu.CompilerParams(vmem_limit_bytes=1 << 20),
    )(gi, gp)
    return gi.reshape(PART, BATCH, CHANS), gp.transpose(1, 0, 2)


def solution(mesh):
    placed = (P("tm", None, None), P(None, None, "freq"), P(None, "freq"), P())
    return jax.shard_map(
        on_device,
        mesh=mesh,
        in_specs=placed,
        out_specs=(P(("tm", "freq"), None, None), P("tm", None, "freq")),
        check_vma=False,
    )
```
